32 devices in a mesh: snap: 2 (over core), brick: 16 (over z, y, x).
Axes of the slice: x: 2, y: 2, z: 4, core: 2. Of those that a mesh axis runs over, the one named last changes fastest.
Arguments:
- atom_features: bfloat16 [2, 32, 262144], P('snap', None, 'brick'), may hold values from -6 to 6
- cotangent: bfloat16 [2, 32, 262144], P('snap', None, 'brick'), may hold values from -6 to 6
- cell_index: int32 [2, 4, 262144], P('snap', None, 'brick'), may hold values from 0 to 39, as said below
- assign_weight: float32 [2, 4, 262144], P('snap', None, 'brick'), may hold values from 0.05 to 1
- conv_kernel: bfloat16 [27, 32, 32], replicated, may hold values from -0.21875 to 0.21875
- spectral_gain: float32 [32, 128, 128], P(None, None, 'brick'), may hold values from 0.1 to 2
Outputs:
- atom_grad: bfloat16 [2, 32, 262144], P('snap', None, 'brick')
- kernel_grad: float32 [27, 32, 32], replicated
- gain_grad: float32 [32, 128, 128], P(None, None, 'brick')
The draws below stay inside these ranges and needn't reach their ends.
Inputs may be any that keep to these rules, and one draw needn't show every extreme that they name: `cell_index`: for each slot there are p from 0 to 8 and z from 0 to 2 such that its four corners are, in order, p * 4 + z, (p + 1) * 4 + z, p * 4 + z + 1 and (p + 1) * 4 + z + 1.
All inputs are finite; a program needn't handle non-finite values.
Results may differ from the reference program's by a relative error of at most 0.0058.
Values may be sent and summed in bfloat16 or wider, within the bound.
A program may use at most 64 MiB of HBM per device.

```python
import math
import jax
import jax.numpy as jnp
from jax import lax

C = 32
NX = 128
NY = 128
NZ = 4
SLOTS = 128
CORNERS = 4
SNAPS = 2
XDEV = 8
ATOM_DEV = 16384
ATOMS = 262144


def draw_cell_index(key, part):
    first_key, second_key = jax.random.split(jax.random.fold_in(key, 17))
    plane_base = jax.random.randint(first_key, (SNAPS, ATOMS), 0, XDEV + 1)
    depth_base = jax.random.randint(second_key, (SNAPS, ATOMS), 0, NZ - 1)
    corners = [plane_base * NZ + depth_base, (plane_base + 1) * NZ + depth_base, plane_base * NZ + depth_base + 1, (plane_base + 1) * NZ + depth_base + 1]
    return jnp.stack(corners, axis=1).astype(jnp.int32)


def level_of(rng, extent, shards, smallest, largest):
    def one(position, shards_of):
        heights = jax.random.uniform(jax.random.fold_in(jax.random.fold_in(rng, 6), position), (shards_of,), jnp.float32, smallest / len(shards), largest / len(shards))
        return jnp.repeat(jnp.exp(heights), extent[position] // shards_of).reshape((-1,) + (1,) * (len(extent) - position - 1))

    level = one(*shards[0])
    for cut in shards[1:]:
        level = level * one(*cut)
    return level


def normal_values(rng, dims, deviation, limit, cuts=(), kind=jnp.bfloat16):
    level = level_of(rng, dims, cuts, -0.22, 0.18) if cuts else 1.0
    drawn = jax.random.normal(rng, dims, jnp.float32) * deviation * level
    return jnp.minimum(jnp.maximum(drawn, -limit), limit).astype(kind)


def setup_inputs(seed: int = 0) -> dict:
    streams_of = jax.random.split(jax.random.key(seed), 7)
    atom_features = normal_values(streams_of[0], (SNAPS, C, ATOMS), 1.0, 6.0, ((0, 2), (2, 16)))
    cotangent = normal_values(streams_of[1], (SNAPS, C, ATOMS), 1.0, 6.0, ((0, 2), (2, 16)))
    cell_index = draw_cell_index(jax.random.fold_in(streams_of[6], 71), 0)
    assign_weight = jnp.clip(0.05 + 0.95 * jax.random.uniform(streams_of[3], (SNAPS, CORNERS, ATOMS), jnp.float32) ** level_of(streams_of[3], (SNAPS, CORNERS, ATOMS), ((0, 2), (2, 16)), -0.2, 0.2), 0.05, 1.0)
    conv_kernel = normal_values(streams_of[4], (27, C, C), (27 * C) ** -0.5, 0.21875)
    spectral_gain = jnp.clip(0.1 + 1.9 * jax.random.uniform(streams_of[5], (C, NX, NY), jnp.float32) ** level_of(streams_of[5], (C, NX, NY), ((2, 16),), -0.2, 0.2), 0.1, 2.0)
    return {"atom_features": atom_features, "cotangent": cotangent, "cell_index": cell_index, "assign_weight": assign_weight, "conv_kernel": conv_kernel, "spectral_gain": spectral_gain}


def offset_list():
    return [(first, second, third) for first in (-1, 0, 1) for second in (-1, 0, 1) for third in (-1, 0, 1)]

def displaced(volume, offsets):
    moved = jnp.roll(volume, (-offsets[0], -offsets[1]), axis=(1, 2))
    if offsets[2] == 1:
        moved = jnp.concatenate([moved[..., 1:], jnp.zeros_like(moved[..., :1])], axis=-1)
    elif offsets[2] == -1:
        moved = jnp.concatenate([jnp.zeros_like(moved[..., :1]), moved[..., :-1]], axis=-1)
    return moved

def rounded(values):
    return lax.optimization_barrier(values.astype(jnp.bfloat16)).astype(jnp.float32)

def reference(atom_features, cotangent, cell_index, assign_weight, conv_kernel, spectral_gain):
    atom_ids = jnp.arange(ATOMS, dtype=jnp.int32)
    brick_of = atom_ids // ATOM_DEV
    row_of = atom_ids % ATOM_DEV // SLOTS
    kernel_f = conv_kernel.astype(jnp.float32)
    offsets_all = offset_list()
    kernel_total = jnp.zeros((27, C, C), jnp.float32)
    gain_total = jnp.zeros((C, NX, NY), jnp.float32)
    results = []
    for snap_id in range(SNAPS):
        weight_bf = rounded(assign_weight[snap_id])
        plane_local = cell_index[snap_id] // NZ
        depth_local = cell_index[snap_id] % NZ
        plane_global = (brick_of[None, :] * XDEV + plane_local - 1) % NX
        flat_cell = ((plane_global * NY + row_of[None, :]) * NZ + depth_local).astype(jnp.int32)
        features = jnp.concatenate([atom_features[snap_id].astype(jnp.float32), cotangent[snap_id].astype(jnp.float32)], axis=0)
        spread = jnp.zeros((2 * C, NX * NY * NZ), jnp.float32)
        for corner in range(CORNERS):
            spread = spread.at[:, flat_cell[corner]].add(weight_bf[corner][None, :] * features)
        spread = spread.reshape(2 * C, NX, NY, NZ)
        state = rounded(spread[:C])
        grad_mesh = spread[C:]
        mixed = state
        for tap, offsets in enumerate(offsets_all):
            mixed = mixed + jnp.einsum('cxyz,cd->dxyz', displaced(state, offsets), kernel_f[tap])
        grad_freq = jnp.fft.fft2(grad_mesh, axes=(1, 2))
        mixed_freq = jnp.fft.fft2(mixed, axes=(1, 2))
        gain_total = gain_total + lax.optimization_barrier(jnp.sum(jnp.real(jnp.conj(grad_freq) * mixed_freq), axis=3))
        grad_mixed = jnp.real(jnp.fft.ifft2(spectral_gain[..., None] * grad_freq, axes=(1, 2)))
        grad_state = rounded(grad_mixed)
        pulled_sum = grad_state
        tap_grads = []
        for tap, offsets in enumerate(offsets_all):
            negated = (-offsets[0], -offsets[1], -offsets[2])
            pulled_sum = pulled_sum + jnp.einsum('dxyz,cd->cxyz', displaced(grad_state, negated), kernel_f[tap])
            tap_grads.append(jnp.einsum('cxyz,dxyz->cd', displaced(state, offsets), grad_state))
        kernel_total = kernel_total + jnp.stack(tap_grads)
        pulled = rounded(pulled_sum).reshape(C, NX * NY * NZ)
        atom_total = jnp.zeros((C, ATOMS), jnp.float32)
        for corner in range(CORNERS):
            atom_total = atom_total + weight_bf[corner][None, :] * pulled[:, flat_cell[corner]]
        results.append(atom_total.astype(jnp.bfloat16))
    kernel_grad = kernel_total / math.sqrt(SNAPS * NX * NY * NZ)
    gain_grad = gain_total / (NX * NY * math.sqrt(SNAPS * NZ))
    return (jnp.stack(results), kernel_grad, gain_grad)
```

```python
import math

import jax
import jax.numpy as jnp
from jax import lax
import numpy as np
from jax.experimental import pallas as pl
from jax.experimental.pallas import tpu as pltpu
from jax.sharding import PartitionSpec as P

NX = 128
NY = 128
NZ = 4
CORNERS = 4


HIGHEST = lax.Precision.HIGHEST


def from_behind(value, axis, steps):
    count = lax.axis_size(axis)
    pairs = [(source, (source + steps) % count) for source in range(count)]
    return lax.ppermute(value, axis, pairs)


def with_halo(cells, sides, width):
    for axis, dim in sides:
        count = lax.axis_size(axis)
        head = lax.slice_in_dim(cells, 0, width, axis=dim)
        tail = lax.slice_in_dim(cells, cells.shape[dim] - width, cells.shape[dim], axis=dim)
        cells = jnp.concatenate(
            [
                lax.ppermute(tail, axis, [(i, (i + 1) % count) for i in range(count)]),
                cells,
                lax.ppermute(head, axis, [((i + 1) % count, i) for i in range(count)]),
            ],
            axis=dim,
        )
    return cells


def tables(length):
    indices = jnp.arange(length, dtype=jnp.int32)
    phases = indices[:, None] * indices[None, :] % length
    angles = phases.astype(jnp.float32) * (2.0 * math.pi / length)
    return (jnp.cos(angles), jnp.sin(angles))


def patches(padded, first_plane, planes):
    row_total = padded.shape[1]
    thickness = padded.shape[3]
    wrapped = jnp.concatenate([padded[:, -1:], padded, padded[:, :1]], axis=1)
    widened = jnp.pad(wrapped, ((0, 0), (0, 0), (0, 0), (1, 1)))
    pieces = []
    for step_first in (-1, 0, 1):
        for step_second in (-1, 0, 1):
            for step_third in (-1, 0, 1):
                pieces.append(
                    widened[
                        :,
                        1 + step_second : 1 + step_second + row_total,
                        first_plane + step_first : first_plane + step_first + planes,
                        1 + step_third : 1 + step_third + thickness,
                    ]
                )
    return jnp.stack(pieces)


def transform_rows(mesh_field, row_cosine, row_sine):
    real_part = jnp.einsum("cyxz,yk->ckxz", mesh_field, row_cosine, precision=HIGHEST)
    imag_part = -jnp.einsum("cyxz,yk->ckxz", mesh_field, row_sine, precision=HIGHEST)
    return jnp.stack([real_part, imag_part])


def transform_columns(stacked, col_cosine, col_sine, sign_value):

    def apply_table(part_values, table):
        return jnp.einsum("ckxz,xq->ckqz", part_values, table, precision=HIGHEST)

    real_part = stacked[0]
    imag_part = stacked[1]
    new_real = apply_table(real_part, col_cosine) + sign_value * apply_table(imag_part, col_sine)
    new_imag = apply_table(imag_part, col_cosine) - sign_value * apply_table(real_part, col_sine)
    return jnp.stack([new_real, new_imag])


def shards(atom_features, cotangent, cell_index, assign_weight, conv_kernel, spectral_gain):
    channels = atom_features.shape[1]
    slot_count = atom_features.shape[2] // NY
    own_planes = NX // lax.axis_size("brick")
    tile_cells = (own_planes + 2) * NZ
    snap_count = lax.axis_size("snap")
    index_tiles = cell_index[0].reshape(CORNERS, NY, slot_count)
    weight_tiles = assign_weight[0].astype(jnp.bfloat16).reshape(CORNERS, NY, slot_count)
    cell_numbers = jnp.arange(tile_cells, dtype=jnp.int32)
    blocks = jnp.zeros((NY, tile_cells, slot_count), jnp.bfloat16)
    for corner in range(CORNERS):
        matches = index_tiles[corner][:, None, :] == cell_numbers[None, :, None]
        blocks = blocks + jnp.where(
            matches, weight_tiles[corner][:, None, :], jnp.zeros((), jnp.bfloat16)
        )
    stacked = jnp.concatenate([atom_features[0], cotangent[0]], axis=0).reshape(
        2 * channels, NY, slot_count
    )
    spread = jnp.einsum("cts,tjs->ctj", stacked, blocks, preferred_element_type=jnp.float32)
    spread = spread.reshape(2 * channels, NY, own_planes + 2, NZ)
    from_above = from_behind(spread[:, :, 0], "brick", -1)
    from_below = from_behind(spread[:, :, own_planes + 1], "brick", 1)
    owned_planes = spread[:, :, 1 : own_planes + 1]
    owned_planes = owned_planes.at[:, :, 0].add(from_below)
    owned_planes = owned_planes.at[:, :, own_planes - 1].add(from_above)
    state_bf = owned_planes[:channels].astype(jnp.bfloat16)
    grad_mesh = owned_planes[channels:]
    col_cosine, col_sine = tables(NX)
    row_cosine, row_sine = tables(NY)

    def make_rows(mesh_field):
        return transform_rows(mesh_field, row_cosine, row_sine)

    def to_columns(part_rows):
        return transform_columns(part_rows, col_cosine, col_sine, 1.0)

    grad_rows = make_rows(grad_mesh)
    grad_spec = to_columns(
        lax.all_to_all(grad_rows, "brick", split_axis=2, concat_axis=3, tiled=True)
    )
    state_rim = with_halo(state_bf, (("brick", 2),), 1)
    state_patch = patches(state_rim, 1, own_planes)
    conv_out = jnp.einsum(
        "tcyxz,tcd->dyxz", state_patch, conv_kernel, preferred_element_type=jnp.float32
    )
    mesh_mixed = state_bf.astype(jnp.float32) + conv_out
    mixed_rows = make_rows(mesh_mixed)
    state_spec = to_columns(
        lax.all_to_all(
            mixed_rows.astype(jnp.bfloat16), "brick", split_axis=2, concat_axis=3, tiled=True
        ).astype(mixed_rows.dtype)
    )
    products = jnp.sum(grad_spec[0] * state_spec[0] + grad_spec[1] * state_spec[1], axis=3)
    gain_part = jnp.transpose(products, (0, 2, 1)) / (NX * NY * math.sqrt(snap_count * NZ))
    gain_local = jnp.transpose(spectral_gain, (0, 2, 1))
    filtered = grad_spec * gain_local[None, :, :, :, None]
    before_cross = transform_columns(filtered, col_cosine, col_sine, -1.0)
    part_cols = lax.all_to_all(before_cross, "brick", split_axis=3, concat_axis=2, tiled=True)
    real_rows = jnp.einsum("ckxz,ky->cyxz", part_cols[0], row_cosine, precision=HIGHEST)
    imag_rows = jnp.einsum("ckxz,ky->cyxz", part_cols[1], row_sine, precision=HIGHEST)
    grad_mixed = (real_rows - imag_rows) / (NX * NY)
    grad_bf = grad_mixed.astype(jnp.bfloat16)
    flipped = conv_kernel[::-1]
    grad_padded = with_halo(grad_bf, (("brick", 2),), 1)
    grad_patch = patches(grad_padded, 1, own_planes)
    back_conv = jnp.einsum(
        "tdyxz,tcd->cyxz", grad_patch, flipped, preferred_element_type=jnp.float32
    )
    pulled = (grad_bf.astype(jnp.float32) + back_conv).astype(jnp.bfloat16)
    pulled_full = with_halo(pulled, (("brick", 2),), 1)
    kernel_part = jnp.einsum(
        "tcyxz,dyxz->tcd", state_patch, grad_bf, preferred_element_type=jnp.float32
    )
    kernel_part = kernel_part / math.sqrt(snap_count * NX * NY * NZ)
    pulled_tiles = pulled_full.reshape(channels, NY, tile_cells)
    atom_total = jnp.einsum(
        "ctj,tjs->cts", pulled_tiles, blocks, preferred_element_type=jnp.float32
    )
    atom_grad = atom_total.astype(jnp.bfloat16).reshape(1, channels, NY * slot_count)
    kernel_grad = lax.psum(kernel_part, ("snap", "brick"))
    gain_grad = lax.psum(gain_part, "snap")
    return (atom_grad, kernel_grad, gain_grad)


BF = jnp.bfloat16
F32 = jnp.float32
LANES = 128
ROWS = 8
PADX = 16
MESH = pl.DeviceIdType.MESH


def contract(left, right, dims, precision=None):
    return lax.dot_general(
        left, right, ((dims[:1], dims[1:]), ((), ())),
        precision=precision, preferred_element_type=F32,
    )


def vmem():
    return pl.BlockSpec(memory_space=pltpu.VMEM)


def shape_of(dims, kind):
    return jax.ShapeDtypeStruct(dims, kind)


def corner_block(index_ref, weight_ref, lanes, cell_of_row):
    block = jnp.zeros(cell_of_row.shape, F32)
    index = index_ref[:, lanes]
    weight = weight_ref[:, lanes]
    for corner in range(CORNERS):
        block = jnp.where(
            index[corner : corner + 1] == cell_of_row, weight[corner : corner + 1], block
        )
    return block.astype(BF)


def row_cells():
    row = lax.broadcasted_iota(jnp.int32, (NZ * PADX, LANES), 0)
    return (row % PADX) * NZ + row // PADX


def run_all(first, total, make):
    def go(step, carry):
        make(step).start()
        return carry

    lax.fori_loop(first, total, go, 0)


def wait_all(first, total, make):
    def finish(step, carry):
        make(step).wait()
        return carry

    lax.fori_loop(first, total, finish, 0)


def split(value):
    high = value.astype(BF)
    return high, (value - high.astype(F32)).astype(BF)


def three(left, right):
    left_high, left_low = left
    right_high, right_low = right
    return (
        contract(left_high, right_high, (1, 0))
        + contract(left_high, right_low, (1, 0))
        + contract(left_low, right_high, (1, 0))
    )


def widen(value):
    return jnp.concatenate(
        [jnp.roll(value, 1, axis=0), value, jnp.roll(value, -1, axis=0)], axis=1
    ).astype(BF)


def whole_body(
    bricks, snaps, chunks,
    feature_hbm, cotangent_hbm, index_hbm, weight_hbm, taps_hbm, gain_hbm,
    order_hbm, rows_hbm, cols_hbm, inv_cols_hbm, inv_rows_hbm,
    atom_ref, kernel_ref, gain_out_ref,
    feature_ref, cotangent_ref, index_ref, weight_ref, taps_ref, gain_ref,
    order_ref, rows_ref, cols_ref, inv_cols_ref, inv_rows_ref,
    blocks, sums, edge, low, high, band, back_band, state, cat, grad_send, mixed_send,
    grad_slab, mixed_slab, gain_slab, field_f, back_f, spectra, ext, ret, back_cat, pulled,
    gain_send, gain_land, kernel_part, kernel_land, kernel_mine, kernel_all,
    edge_send, edge_recv, out_send, out_recv, ret_send, ret_recv,
    gain_ssem, gain_rsem, red_send, red_recv, in_sem, table_sem,
):
    channels = feature_ref.shape[0]
    planes = NX // bricks
    per = channels // bricks
    total = bricks * snaps
    me = lax.axis_index("brick")
    side = lax.axis_index("snap")
    flat = side * bricks + me
    above = lax.rem(me + 1, bricks)
    below = lax.rem(me + bricks - 1, bricks)
    barrier = pltpu.get_barrier_semaphore()

    def device_of(step):
        other = lax.rem(flat + step, total)
        return other, {"snap": other // bricks, "brick": lax.rem(other, bricks)}

    def hello(step, carry):
        pl.semaphore_signal(barrier, inc=1, device_id=device_of(step)[1], device_id_type=MESH)
        return carry

    def remote(src, dst, send_sem, recv_sem, device):
        return pltpu.make_async_remote_copy(
            src_ref=src, dst_ref=dst, send_sem=send_sem, recv_sem=recv_sem,
            device_id=device, device_id_type=MESH,
        )

    half = bricks // 2

    def partner(slot):
        near = slot // half
        offset = slot + near * (1 - half)
        return lax.rem(me // half + 1 - near, 2) * half + lax.rem(me + offset, half)

    span = NY // chunks
    tables = [
        pltpu.make_async_copy(src, dst, table_sem.at[number])
        for number, (src, dst) in enumerate(
            [
                (gain_hbm, gain_ref), (order_hbm, order_ref), (taps_hbm, taps_ref),
                (rows_hbm, rows_ref), (cols_hbm, cols_ref), (inv_cols_hbm, inv_cols_ref),
                (inv_rows_hbm, inv_rows_ref),
            ]
        )
    ]
    loads = []
    for chunk in range(chunks):
        lanes = pl.ds(chunk * span * LANES, span * LANES)
        loads.append(
            [
                pltpu.make_async_copy(src.at[:, lanes], dst.at[:, lanes], in_sem.at[number, chunk])
                for number, (src, dst) in enumerate(
                    [
                        (index_hbm, index_ref), (weight_hbm, weight_ref),
                        (feature_hbm, feature_ref), (cotangent_hbm, cotangent_ref),
                    ]
                )
            ]
        )
    for load in loads[0]:
        load.start()
    lax.fori_loop(1, total, hello, 0)
    for group in loads[1:]:
        for load in group:
            load.start()
    for load in tables:
        load.start()

    cells = row_cells()

    def spread_step(step, carry):
        parts = [[], []]
        for q in range(ROWS):
            y = step * ROWS + q
            lanes = pl.ds(pl.multiple_of(y * LANES, LANES), LANES)
            block = corner_block(index_ref, weight_ref, lanes, cells)
            blocks[y] = block
            stacked = jnp.concatenate([feature_ref[:, lanes], cotangent_ref[:, lanes]], axis=0)
            found = contract(block, stacked, (1, 1))
            for f in range(2):
                parts[f].append(
                    jnp.concatenate(
                        [
                            found[z * PADX : (z + 1) * PADX, f * channels : (f + 1) * channels]
                            for z in range(NZ)
                        ],
                        axis=1,
                    )
                )
        for f in range(2):
            turned = jnp.transpose(jnp.stack(parts[f]), (1, 0, 2))
            sums[f, :, pl.ds(pl.multiple_of(step * ROWS, ROWS), ROWS), :] = turned[: planes + 2]
        return carry

    def gain_copy(slot):
        target = partner(slot)
        return remote(
            gain_ref.at[pl.ds(target * per, per)], gain_slab.at[:, me],
            out_send.at[2, slot], out_recv.at[2, slot], {"brick": target},
        )

    def edge_copy(field, way):
        first, count = (3 * way, 2) if field == 0 else (3 * way + 2, 1)
        land = low if way == 0 else high
        return remote(
            edge.at[pl.ds(first, count)], land.at[pl.ds(first - 3 * way, count)],
            edge_send.at[way, field], edge_recv.at[way, field],
            {"brick": above if way == 0 else below},
        )

    for chunk in range(chunks):
        for load in loads[chunk]:
            load.wait()
        if chunk == chunks - 1:
            pl.semaphore_wait(barrier, total - 1)
            tables[0].wait()
            run_all(0, bricks - 1, gain_copy)
        lax.fori_loop(chunk * (span // ROWS), (chunk + 1) * (span // ROWS), spread_step, 0)
    for slot, (f, plane) in enumerate(
        [(0, planes), (0, planes + 1), (1, planes + 1), (0, 0), (0, 1), (1, 0)]
    ):
        edge[slot] = sums[f, plane].astype(BF)
    for field in (1, 0):
        for way in range(2):
            edge_copy(field, way).start()

    gain_slab[:, me] = gain_ref[pl.ds(me * per, per)]
    tables[1].wait()
    order = order_ref[...]
    inner = planes - 2

    def place(field, out, slot):
        turned = contract(order, field.astype(BF), (1, 1))
        out[slot] = turned.reshape(out.shape[1:]).astype(BF)

    def field_copy(kind, send, slab, first, count):
        def make(slot):
            target = partner(slot)
            return remote(
                send.at[pl.ds(first, count), target],
                slab.at[pl.ds(me * planes + first, count)],
                out_send.at[kind, slot], out_recv.at[kind, slot], {"brick": target},
            )

        return make

    grad_inner = field_copy(0, grad_send, grad_slab, 0, inner)
    grad_outer = field_copy(3, grad_send, grad_slab, inner, 2)
    mixed_copy = field_copy(1, mixed_send, mixed_slab, 0, planes)
    slots = [inner] + list(range(inner)) + [inner + 1]

    for plane in range(1, planes - 1):
        place(sums[1, plane + 1], grad_send, slots[plane])
    run_all(0, bricks - 1, grad_inner)

    tables[2].wait()
    lane = lax.broadcasted_iota(jnp.int32, (channels, LANES), 1) // channels
    for dx in range(3):
        for dy in range(3):
            tiled = []
            for dz in range(3):
                tap = taps_ref[9 * dx + 3 * dy + dz].astype(F32)
                tiled.append(jnp.concatenate([tap] * NZ, axis=1))
            lines = []
            for z in range(NZ):
                line = jnp.zeros((channels, LANES), F32)
                for dz in range(3):
                    line = jnp.where(lane == z - (dz - 1), tiled[dz], line)
                lines.append(line)
            square = jnp.concatenate(lines, axis=0)
            band[dx, dy * LANES : (dy + 1) * LANES, :] = square.astype(BF)
            back_band[2 - dx, (2 - dy) * LANES : (3 - dy) * LANES, :] = jnp.transpose(
                square, (1, 0)
            ).astype(BF)

    for way in range(2):
        edge_copy(1, way).wait()
    place(sums[1, 1] + low[2].astype(F32), grad_send, slots[0])
    place(sums[1, planes] + high[2].astype(F32), grad_send, slots[planes - 1])
    run_all(0, bricks - 1, grad_outer)
    grad_slab[pl.ds(me * planes, planes)] = grad_send[:, me]

    for way in range(2):
        edge_copy(0, way).wait()
    for plane in range(planes + 2):
        value = sums[0, plane]
        if plane < 2:
            value = value + low[plane].astype(F32)
        if plane >= planes:
            value = value + high[plane - planes].astype(F32)
        rounded = value.astype(BF)
        state[plane] = rounded
        cat[plane] = widen(rounded.astype(F32))
    for plane in range(planes):
        value = state[plane + 1].astype(F32)
        for dx in range(3):
            value = value + contract(cat[plane + dx], band[dx], (1, 0))
        place(value, mixed_send, slots[plane])
    mixed_slab[pl.ds(me * planes, planes)] = mixed_send[:, me]
    for load in tables[3:]:
        load.wait()

    rows = rows_ref[...]
    cols = (cols_ref[0], cols_ref[1])
    inv_cols = (inv_cols_ref[0], inv_cols_ref[1])
    inv_rows = (inv_rows_ref[0], inv_rows_ref[1])

    def transform(channel):
        tall = jnp.concatenate([field_f[:, z * per + channel, :] for z in range(NZ)], axis=0)
        tall = tall.astype(BF)
        first = contract(jnp.concatenate([tall, tall], axis=1), rows, (1, 0))
        halves = []
        for half in range(2):
            halves.append(
                jnp.concatenate(
                    [
                        first[z * NX : (z + 1) * NX, half * NY : (half + 1) * NY]
                        for z in range(NZ)
                    ],
                    axis=1,
                )
            )
        return three(cols, split(jnp.concatenate(halves, axis=0)))

    wait_all(0, bricks - 1, gain_copy)
    wait_all(0, bricks - 1, grad_inner)
    wait_all(0, bricks - 1, grad_outer)
    field_f[...] = grad_slab[...].astype(F32)
    for channel in range(per):
        spectra[channel] = transform(channel)
        gain = jnp.transpose(gain_slab[channel].reshape(NY, NX), (1, 0))
        gain = jnp.concatenate([gain] * NZ, axis=1)
        gain = jnp.concatenate([gain, gain], axis=0)
        back = three(inv_cols, split(spectra[channel] * gain))
        flats = []
        for z in range(NZ):
            piece = back[:, z * NY : (z + 1) * NY]
            flats.append(jnp.concatenate([piece[:NX], piece[NX:]], axis=1))
        out = three(split(jnp.concatenate(flats, axis=0)), inv_rows) * (1.0 / (NX * NY))
        for z in range(NZ):
            back_f[:, z * per + channel, :] = out[z * NX : (z + 1) * NX]
    ext[pl.ds(2, NX)] = back_f[...].astype(BF)
    ext[pl.ds(0, 2)] = back_f[pl.ds(NX - 2, 2)].astype(BF)
    ext[pl.ds(NX + 2, 2)] = back_f[pl.ds(0, 2)].astype(BF)

    def ret_copy(slot):
        target = partner(slot)
        return remote(
            ext.at[pl.ds(target * planes, planes + 4)], ret.at[:, me],
            ret_send.at[slot], ret_recv.at[slot], {"brick": target},
        )

    run_all(0, bricks - 1, ret_copy)
    run_all(0, bricks - 1, mixed_copy)
    ret[:, me] = ext[pl.ds(me * planes, planes + 4)]
    wait_all(0, bricks - 1, ret_copy)

    for plane in range(planes + 4):
        field = ret[plane].astype(F32).reshape(LANES, NY).astype(BF)
        back_cat[plane] = widen(contract(field, order, (0, 0)))
    own = back_cat[pl.ds(2, planes)].reshape(planes * NY, 3 * LANES)
    groups = [jnp.zeros((channels, LANES), F32) for _ in range(kernel_all.shape[0] * ROWS // channels)]
    tap_scale = 1.0 / math.sqrt(snaps * NX * NY * NZ)
    for dx in range(3):
        near = state[pl.ds(dx, planes)].reshape(planes * NY, LANES)
        gram = contract(near, own, (0, 0))
        for dy in range(3):
            square = gram[:, (2 - dy) * LANES : (3 - dy) * LANES]
            for dz in range(3):
                line = jnp.zeros((channels, LANES), F32)
                for z in range(NZ):
                    source = z + dz - 1
                    if 0 <= source < NZ:
                        line = jnp.where(
                            lane == z, square[source * channels : (source + 1) * channels], line
                        )
                line = line + pltpu.roll(line, LANES // 2, 1)
                line = line + pltpu.roll(line, LANES // 4, 1)
                tap = 9 * dx + 3 * dy + dz
                groups[tap // NZ] = jnp.where(
                    lane == tap % NZ, line * tap_scale, groups[tap // NZ]
                )
    tiles = channels // ROWS
    for position, value in enumerate(groups):
        kernel_part[position * tiles : (position + 1) * tiles] = value.reshape(tiles, ROWS, LANES)

    def scatter(step):
        other, device = device_of(step)
        return remote(
            kernel_part.at[other], kernel_land.at[flat],
            red_send.at[0, step], red_recv.at[0, step], device,
        )

    def share(step):
        _, device = device_of(step)
        return remote(
            kernel_mine, kernel_all.at[flat],
            red_send.at[1, step], red_recv.at[1, step], device,
        )

    run_all(1, total, scatter)
    kernel_land[flat] = kernel_part[flat]

    for plane in range(planes + 2):
        value = back_cat[plane + 1, :, LANES : 2 * LANES].astype(F32)
        for dx in range(3):
            value = value + contract(back_cat[plane + dx], back_band[dx], (1, 0))
        pulled[plane] = value.astype(BF).astype(F32)
    for plane in range(planes + 2, PADX):
        pulled[plane] = jnp.zeros((NY, LANES), F32)

    def gather_step(step, carry):
        here = pl.ds(pl.multiple_of(step * ROWS, ROWS), ROWS)
        turned = jnp.transpose(pulled[:, here, :], (1, 0, 2))
        for q in range(ROWS):
            y = step * ROWS + q
            lanes = pl.ds(pl.multiple_of(y * LANES, LANES), LANES)
            plane = turned[q]
            tall = jnp.concatenate(
                [plane[:, z * channels : (z + 1) * channels] for z in range(NZ)], axis=0
            )
            atom_ref[:, lanes] = contract(tall.astype(BF), blocks[y], (0, 0)).astype(BF)
        return carry

    steps = NY // ROWS
    lax.fori_loop(0, steps // 2, gather_step, 0)

    wait_all(0, bricks - 1, mixed_copy)
    field_f[...] = mixed_slab[...].astype(F32)
    scale = 1.0 / (NX * NY * math.sqrt(snaps * NZ))
    for channel in range(per):
        product = spectra[channel] * transform(channel)
        product = product[:NX] + product[NX:]
        part = product[:, :NY]
        for z in range(1, NZ):
            part = part + product[:, z * NY : (z + 1) * NY]
        part = jnp.transpose(part * scale, (1, 0))
        gain_send[channel] = part.reshape(gain_send.shape[1:]).astype(gain_send.dtype)

    def part_copy(step):
        other, device = device_of(step)
        return remote(
            gain_send.at[:, lax.rem(other, bricks)], gain_land.at[side, pl.ds(me * per, per)],
            gain_ssem.at[step], gain_rsem.at[step], device,
        )

    run_all(1, total, part_copy)
    gain_land[side, pl.ds(me * per, per)] = gain_send[:, me]

    wait_all(1, total, scatter)
    kernel_mine[...] = jnp.sum(kernel_land[...], axis=0)
    run_all(1, total, share)
    kernel_all[flat] = kernel_mine[...]

    lax.fori_loop(steps // 2, steps, gather_step, 0)

    wait_all(1, total, part_copy)
    gain_sum = gain_land[0].astype(F32)
    for other in range(1, snaps):
        gain_sum = gain_sum + gain_land[other].astype(F32)
    gain_out_ref[...] = gain_sum
    wait_all(1, total, share)
    final = kernel_all[...].reshape(kernel_all.shape[0] * ROWS // channels, channels, LANES)
    for tap in range(kernel_ref.shape[0]):
        at = (tap % NZ) * channels
        kernel_ref[tap] = final[tap // NZ][:, at : at + channels]


def fast_shards(sizes, atom_features, cotangent, cell_index, assign_weight, conv_kernel, spectral_gain):
    snaps, bricks = sizes
    channels, atoms = atom_features.shape[1:]
    planes = NX // bricks
    per = channels // bricks
    group = NZ * per
    total = bricks * snaps
    chunks = 4
    order = np.zeros((LANES, LANES), np.float32)
    for brick in range(bricks):
        for z in range(NZ):
            for c in range(per):
                order[brick * group + z * per + c, z * channels + brick * per + c] = 1.0

    def angles(length):
        phase = np.outer(np.arange(length), np.arange(length)) % length
        turn = 2.0 * np.pi * phase / length
        return np.cos(turn), np.sin(turn)

    def halves(table):
        table = np.asarray(table, np.float32)
        high = table.astype(BF)
        low = (table - high.astype(np.float32)).astype(BF)
        return high, low

    col_cos, col_sin = angles(NX)
    row_cos, row_sin = angles(NY)
    rows = jnp.asarray(np.concatenate(halves(np.concatenate([row_cos, -row_sin], axis=1)), axis=0))
    local = list(range(1, planes - 1)) + [0, planes - 1]
    order_x = [brick * planes + plane for brick in range(bricks) for plane in local]
    col_cos_x, col_sin_x = col_cos[:, order_x], col_sin[:, order_x]
    cols = jnp.asarray(np.stack(halves(np.block([[col_cos_x, col_sin_x], [-col_sin_x, col_cos_x]]))))
    inv_cols = jnp.asarray(np.stack(halves(np.block([[col_cos, -col_sin], [col_sin, col_cos]]))))
    inv_rows = jnp.asarray(np.stack(halves(np.concatenate([row_cos, -row_sin], axis=0))))
    mesh_plane = (NY, LANES)
    send = (planes, bricks, group, NY)
    slab = (NX, group, NY)
    piece = (bricks, NY // bricks, NX)
    scratch = [
        ((channels, atoms), BF),
        ((channels, atoms), BF),
        ((CORNERS, atoms), jnp.int32),
        ((CORNERS, atoms), F32),
        (conv_kernel.shape, BF),
        ((channels,) + piece[1:], F32),
        (order.shape, BF),
        (rows.shape, BF),
        (cols.shape, BF),
        (inv_cols.shape, BF),
        (inv_rows.shape, BF),
        ((NY, NZ * PADX, LANES), BF),
        ((2, planes + 2) + mesh_plane, F32),
        ((6,) + mesh_plane, BF),
        ((3,) + mesh_plane, BF),
        ((3,) + mesh_plane, BF),
        ((3, 3 * LANES, LANES), BF),
        ((3, 3 * LANES, LANES), BF),
        ((planes + 2,) + mesh_plane, BF),
        ((planes + 2, NY, 3 * LANES), BF),
        (send, BF),
        (send, BF),
        (slab, BF),
        (slab, BF),
        ((per,) + piece, F32),
        (slab, F32),
        (slab, F32),
        ((per, 2 * NX, NZ * NY), F32),
        ((NX + 4, group, NY), BF),
        ((planes + 4, bricks, group, NY), BF),
        ((planes + 4, NY, 3 * LANES), BF),
        ((PADX,) + mesh_plane, F32),
        ((per,) + piece, BF),
        ((snaps, channels) + piece[1:], BF),
        ((total, ROWS, LANES), F32),
        ((total, ROWS, LANES), F32),
        ((ROWS, LANES), F32),
        ((total, ROWS, LANES), F32),
    ]
    sems = [(2, 2)] * 2 + [(4, bricks)] * 2 + [(bricks,)] * 2 + [(total,)] * 2 + [(2, total)] * 2
    sems = sems + [(4, chunks), (7,)]
    atom_grad, kernel_grad, gain_grad = pl.pallas_call(
        lambda *refs: whole_body(bricks, snaps, chunks, *refs),
        out_shape=[
            pltpu.VMEM((channels, atoms), BF),
            pltpu.VMEM(conv_kernel.shape, F32),
            pltpu.VMEM((channels,) + piece[1:], F32),
        ],
        in_specs=[pl.BlockSpec(memory_space=pl.ANY)] * 11,
        out_specs=[vmem()] * 3,
        scratch_shapes=[pltpu.VMEM(dims, kind) for dims, kind in scratch]
        + [pltpu.SemaphoreType.DMA(dims) for dims in sems],
        compiler_params=pltpu.CompilerParams(
            collective_id=1, has_side_effects=True, vmem_limit_bytes=60 * 1024 * 1024
        ),
    )(
        atom_features[0], cotangent[0], cell_index[0], assign_weight[0], conv_kernel,
        jnp.transpose(spectral_gain, (0, 2, 1)), jnp.asarray(order, BF), rows, cols,
        inv_cols, inv_rows,
    )
    return (atom_grad[None], kernel_grad, jnp.transpose(gain_grad, (0, 2, 1)))


def fits(mesh, channels, atoms):
    bricks = mesh.shape["brick"]
    snaps = mesh.shape["snap"]
    return (
        channels * NZ == LANES
        and NX == LANES
        and NY == LANES
        and atoms // bricks == NY * LANES
        and channels % bricks == 0
        and bricks % 2 == 0
        and NZ * channels // bricks == ROWS
        and NX // bricks == ROWS
        and 8 * channels == bricks * snaps * ROWS
    )


def solution(mesh):
    placed = (
        P("snap", None, "brick"),
        P("snap", None, "brick"),
        P("snap", None, "brick"),
        P("snap", None, "brick"),
        P(),
        P(None, None, "brick"),
    )
    sizes = (mesh.shape["snap"], mesh.shape["brick"])

    def pick(*arguments):
        if fits(mesh, arguments[0].shape[1], arguments[0].shape[2] * sizes[1]):
            return fast_shards(sizes, *arguments)
        return shards(*arguments)

    return jax.shard_map(
        pick,
        mesh=mesh,
        in_specs=placed,
        out_specs=(P("snap", None, "brick"), P(), P(None, None, "brick")),
        check_vma=False,
    )
```

```python
import math

import jax
import jax.numpy as jnp
from jax import lax
import numpy as np
from jax.experimental import pallas as pl
from jax.experimental.pallas import tpu as pltpu
from jax.sharding import PartitionSpec as P

NX = 128
NY = 128
NZ = 4
CORNERS = 4


HIGHEST = lax.Precision.HIGHEST


def from_behind(value, axis, steps):
    count = lax.axis_size(axis)
    pairs = [(source, (source + steps) % count) for source in range(count)]
    return lax.ppermute(value, axis, pairs)


def with_halo(cells, sides, width):
    for axis, dim in sides:
        count = lax.axis_size(axis)
        head = lax.slice_in_dim(cells, 0, width, axis=dim)
        tail = lax.slice_in_dim(cells, cells.shape[dim] - width, cells.shape[dim], axis=dim)
        cells = jnp.concatenate(
            [
                lax.ppermute(tail, axis, [(i, (i + 1) % count) for i in range(count)]),
                cells,
                lax.ppermute(head, axis, [((i + 1) % count, i) for i in range(count)]),
            ],
            axis=dim,
        )
    return cells


def tables(length):
    indices = jnp.arange(length, dtype=jnp.int32)
    phases = indices[:, None] * indices[None, :] % length
    angles = phases.astype(jnp.float32) * (2.0 * math.pi / length)
    return (jnp.cos(angles), jnp.sin(angles))


def patches(padded, first_plane, planes):
    row_total = padded.shape[1]
    thickness = padded.shape[3]
    wrapped = jnp.concatenate([padded[:, -1:], padded, padded[:, :1]], axis=1)
    widened = jnp.pad(wrapped, ((0, 0), (0, 0), (0, 0), (1, 1)))
    pieces = []
    for step_first in (-1, 0, 1):
        for step_second in (-1, 0, 1):
            for step_third in (-1, 0, 1):
                pieces.append(
                    widened[
                        :,
                        1 + step_second : 1 + step_second + row_total,
                        first_plane + step_first : first_plane + step_first + planes,
                        1 + step_third : 1 + step_third + thickness,
                    ]
                )
    return jnp.stack(pieces)


def transform_rows(mesh_field, row_cosine, row_sine):
    real_part = jnp.einsum("cyxz,yk->ckxz", mesh_field, row_cosine, precision=HIGHEST)
    imag_part = -jnp.einsum("cyxz,yk->ckxz", mesh_field, row_sine, precision=HIGHEST)
    return jnp.stack([real_part, imag_part])


def transform_columns(stacked, col_cosine, col_sine, sign_value):

    def apply_table(part_values, table):
        return jnp.einsum("ckxz,xq->ckqz", part_values, table, precision=HIGHEST)

    real_part = stacked[0]
    imag_part = stacked[1]
    new_real = apply_table(real_part, col_cosine) + sign_value * apply_table(imag_part, col_sine)
    new_imag = apply_table(imag_part, col_cosine) - sign_value * apply_table(real_part, col_sine)
    return jnp.stack([new_real, new_imag])


def shards(atom_features, cotangent, cell_index, assign_weight, conv_kernel, spectral_gain):
    channels = atom_features.shape[1]
    slot_count = atom_features.shape[2] // NY
    own_planes = NX // lax.axis_size("brick")
    tile_cells = (own_planes + 2) * NZ
    snap_count = lax.axis_size("snap")
    index_tiles = cell_index[0].reshape(CORNERS, NY, slot_count)
    weight_tiles = assign_weight[0].astype(jnp.bfloat16).reshape(CORNERS, NY, slot_count)
    cell_numbers = jnp.arange(tile_cells, dtype=jnp.int32)
    blocks = jnp.zeros((NY, tile_cells, slot_count), jnp.bfloat16)
    for corner in range(CORNERS):
        matches = index_tiles[corner][:, None, :] == cell_numbers[None, :, None]
        blocks = blocks + jnp.where(
            matches, weight_tiles[corner][:, None, :], jnp.zeros((), jnp.bfloat16)
        )
    stacked = jnp.concatenate([atom_features[0], cotangent[0]], axis=0).reshape(
        2 * channels, NY, slot_count
    )
    spread = jnp.einsum("cts,tjs->ctj", stacked, blocks, preferred_element_type=jnp.float32)
    spread = spread.reshape(2 * channels, NY, own_planes + 2, NZ)
    from_above = from_behind(spread[:, :, 0], "brick", -1)
    from_below = from_behind(spread[:, :, own_planes + 1], "brick", 1)
    owned_planes = spread[:, :, 1 : own_planes + 1]
    owned_planes = owned_planes.at[:, :, 0].add(from_below)
    owned_planes = owned_planes.at[:, :, own_planes - 1].add(from_above)
    state_bf = owned_planes[:channels].astype(jnp.bfloat16)
    grad_mesh = owned_planes[channels:]
    col_cosine, col_sine = tables(NX)
    row_cosine, row_sine = tables(NY)

    def make_rows(mesh_field):
        return transform_rows(mesh_field, row_cosine, row_sine)

    def to_columns(part_rows):
        return transform_columns(part_rows, col_cosine, col_sine, 1.0)

    grad_rows = make_rows(grad_mesh)
    grad_spec = to_columns(
        lax.all_to_all(grad_rows, "brick", split_axis=2, concat_axis=3, tiled=True)
    )
    state_rim = with_halo(state_bf, (("brick", 2),), 1)
    state_patch = patches(state_rim, 1, own_planes)
    conv_out = jnp.einsum(
        "tcyxz,tcd->dyxz", state_patch, conv_kernel, preferred_element_type=jnp.float32
    )
    mesh_mixed = state_bf.astype(jnp.float32) + conv_out
    mixed_rows = make_rows(mesh_mixed)
    state_spec = to_columns(
        lax.all_to_all(
            mixed_rows.astype(jnp.bfloat16), "brick", split_axis=2, concat_axis=3, tiled=True
        ).astype(mixed_rows.dtype)
    )
    products = jnp.sum(grad_spec[0] * state_spec[0] + grad_spec[1] * state_spec[1], axis=3)
    gain_part = jnp.transpose(products, (0, 2, 1)) / (NX * NY * math.sqrt(snap_count * NZ))
    gain_local = jnp.transpose(spectral_gain, (0, 2, 1))
    filtered = grad_spec * gain_local[None, :, :, :, None]
    before_cross = transform_columns(filtered, col_cosine, col_sine, -1.0)
    part_cols = lax.all_to_all(before_cross, "brick", split_axis=3, concat_axis=2, tiled=True)
    real_rows = jnp.einsum("ckxz,ky->cyxz", part_cols[0], row_cosine, precision=HIGHEST)
    imag_rows = jnp.einsum("ckxz,ky->cyxz", part_cols[1], row_sine, precision=HIGHEST)
    grad_mixed = (real_rows - imag_rows) / (NX * NY)
    grad_bf = grad_mixed.astype(jnp.bfloat16)
    flipped = conv_kernel[::-1]
    grad_padded = with_halo(grad_bf, (("brick", 2),), 1)
    grad_patch = patches(grad_padded, 1, own_planes)
    back_conv = jnp.einsum(
        "tdyxz,tcd->cyxz", grad_patch, flipped, preferred_element_type=jnp.float32
    )
    pulled = (grad_bf.astype(jnp.float32) + back_conv).astype(jnp.bfloat16)
    pulled_full = with_halo(pulled, (("brick", 2),), 1)
    kernel_part = jnp.einsum(
        "tcyxz,dyxz->tcd", state_patch, grad_bf, preferred_element_type=jnp.float32
    )
    kernel_part = kernel_part / math.sqrt(snap_count * NX * NY * NZ)
    pulled_tiles = pulled_full.reshape(channels, NY, tile_cells)
    atom_total = jnp.einsum(
        "ctj,tjs->cts", pulled_tiles, blocks, preferred_element_type=jnp.float32
    )
    atom_grad = atom_total.astype(jnp.bfloat16).reshape(1, channels, NY * slot_count)
    kernel_grad = lax.psum(kernel_part, ("snap", "brick"))
    gain_grad = lax.psum(gain_part, "snap")
    return (atom_grad, kernel_grad, gain_grad)


BF = jnp.bfloat16
F32 = jnp.float32
LANES = 128
ROWS = 8
PADX = 16
MESH = pl.DeviceIdType.MESH


def contract(left, right, dims, precision=None):
    return lax.dot_general(
        left, right, ((dims[:1], dims[1:]), ((), ())),
        precision=precision, preferred_element_type=F32,
    )


def vmem():
    return pl.BlockSpec(memory_space=pltpu.VMEM)


def shape_of(dims, kind):
    return jax.ShapeDtypeStruct(dims, kind)


def corner_block(index_ref, weight_ref, lanes, cell_of_row):
    block = jnp.zeros(cell_of_row.shape, F32)
    index = index_ref[:, lanes]
    weight = weight_ref[:, lanes]
    for corner in range(CORNERS):
        block = jnp.where(
            index[corner : corner + 1] == cell_of_row, weight[corner : corner + 1], block
        )
    return block.astype(BF)


def row_cells():
    row = lax.broadcasted_iota(jnp.int32, (NZ * PADX, LANES), 0)
    return (row % PADX) * NZ + row // PADX


def run_all(first, total, make):
    def go(step, carry):
        make(step).start()
        return carry

    lax.fori_loop(first, total, go, 0)


def wait_all(first, total, make):
    def finish(step, carry):
        make(step).wait()
        return carry

    lax.fori_loop(first, total, finish, 0)


def split(value):
    high = value.astype(BF)
    return high, (value - high.astype(F32)).astype(BF)


def three(left, right):
    left_high, left_low = left
    right_high, right_low = right
    return (
        contract(left_high, right_high, (1, 0))
        + contract(left_high, right_low, (1, 0))
        + contract(left_low, right_high, (1, 0))
    )


def widen(value):
    return jnp.concatenate(
        [jnp.roll(value, 1, axis=0), value, jnp.roll(value, -1, axis=0)], axis=1
    ).astype(BF)


def whole_body(
    bricks, snaps, chunks,
    feature_hbm, cotangent_hbm, index_hbm, weight_hbm, taps_hbm, gain_hbm,
    order_hbm, rows_hbm, cols_hbm, inv_cols_hbm, inv_rows_hbm,
    atom_ref, kernel_ref, gain_out_ref,
    feature_ref, cotangent_ref, index_ref, weight_ref, taps_ref, gain_ref,
    order_ref, rows_ref, cols_ref, inv_cols_ref, inv_rows_ref,
    blocks, sums, edge, low, high, band, back_band, state, cat, grad_send, mixed_send,
    grad_slab, mixed_slab, gain_slab, field_f, back_f, spectra, ext, ret, back_cat, pulled,
    gain_out, gain_send, gain_pair, gain_both, gain_land,
    kernel_part, kernel_pair, kernel_both, kernel_land, kernel_mine, kernel_all,
    edge_sems, grad_sems, mixed_sems, gain_sems, ret_sems, part_sems, pair_sems, red_sems,
    in_sem, table_sem,
):
    channels = feature_ref.shape[0]
    planes = NX // bricks
    per = channels // bricks
    total = bricks * snaps
    me = lax.axis_index("brick")
    side = lax.axis_index("snap")
    flat = side * bricks + me
    above = lax.rem(me + 1, bricks)
    below = lax.rem(me + bricks - 1, bricks)
    barrier = pltpu.get_barrier_semaphore()

    def device_of(step):
        other = lax.rem(flat + step, total)
        return other, {"snap": other // bricks, "brick": lax.rem(other, bricks)}

    def hello(step, carry):
        pl.semaphore_signal(barrier, inc=1, device_id=device_of(step)[1], device_id_type=MESH)
        return carry

    def remote(src, dst, send_sem, recv_sem, device):
        return pltpu.make_async_remote_copy(
            src_ref=src, dst_ref=dst, send_sem=send_sem, recv_sem=recv_sem,
            device_id=device, device_id_type=MESH,
        )

    def partner(slot):
        return lax.rem(me + 1 + slot, bricks)

    def wait_for(src, dst, sems):
        remote(src, dst, sems[0], sems[1], {"brick": above}).wait()

    others = pl.ds(0, bricks - 1)
    span = NY // chunks
    tables = [
        pltpu.make_async_copy(src, dst, table_sem.at[number])
        for number, (src, dst) in enumerate(
            [
                (gain_hbm, gain_ref), (order_hbm, order_ref), (taps_hbm, taps_ref),
                (rows_hbm, rows_ref), (cols_hbm, cols_ref), (inv_cols_hbm, inv_cols_ref),
                (inv_rows_hbm, inv_rows_ref),
            ]
        )
    ]
    loads = []
    for chunk in range(chunks):
        lanes = pl.ds(chunk * span * LANES, span * LANES)
        loads.append(
            [
                pltpu.make_async_copy(src.at[:, lanes], dst.at[:, lanes], in_sem.at[number, chunk])
                for number, (src, dst) in enumerate(
                    [
                        (index_hbm, index_ref), (weight_hbm, weight_ref),
                        (feature_hbm, feature_ref), (cotangent_hbm, cotangent_ref),
                    ]
                )
            ]
        )
    for load in loads[0]:
        load.start()
    lax.fori_loop(1, total, hello, 0)
    for load in loads[1]:
        load.start()

    cells = row_cells()

    def spread_step(step, carry):
        parts = [[], []]
        for q in range(ROWS):
            y = step * ROWS + q
            lanes = pl.ds(pl.multiple_of(y * LANES, LANES), LANES)
            block = corner_block(index_ref, weight_ref, lanes, cells)
            blocks[y] = block
            stacked = jnp.concatenate([feature_ref[:, lanes], cotangent_ref[:, lanes]], axis=0)
            found = contract(block, stacked, (1, 1))
            for f in range(2):
                parts[f].append(
                    jnp.concatenate(
                        [
                            found[z * PADX : (z + 1) * PADX, f * channels : (f + 1) * channels]
                            for z in range(NZ)
                        ],
                        axis=1,
                    )
                )
        for f in range(2):
            turned = jnp.transpose(jnp.stack(parts[f]), (1, 0, 2))
            sums[f, :, pl.ds(pl.multiple_of(step * ROWS, ROWS), ROWS), :] = turned[: planes + 2]
        return carry

    def gain_copy(slot):
        target = partner(slot)
        return remote(
            gain_out.at[pl.ds(target * per, per)], gain_slab.at[:, me],
            gain_sems.at[0], gain_sems.at[1], {"brick": target},
        )

    def edge_copy(way):
        return remote(
            edge.at[pl.ds(2 * way, 2)], low if way == 0 else high,
            edge_sems.at[way, 0], edge_sems.at[way, 1], {"brick": above if way == 0 else below},
        )

    for chunk in range(chunks):
        for load in loads[chunk]:
            load.wait()
        if chunk + 2 < chunks:
            for load in loads[chunk + 2]:
                load.start()
        if chunk + 2 == chunks:
            for load in tables:
                load.start()
        if chunk == chunks - 1:
            tables[0].wait()
            gain_out[...] = gain_ref[...].astype(BF)
            gain_slab[:, me] = gain_out[pl.ds(me * per, per)]
            pl.semaphore_wait(barrier, total - 1)
            run_all(0, bricks - 1, gain_copy)
        lax.fori_loop(chunk * (span // ROWS), (chunk + 1) * (span // ROWS), spread_step, 0)
    for slot, plane in enumerate([planes, planes + 1, 0, 1]):
        edge[slot] = sums[0, plane].astype(BF)

    for way in range(2):
        edge_copy(way).start()
    tables[1].wait()
    order = order_ref[...]

    def place(field, out, plane):
        turned = contract(order, field.astype(BF), (1, 1))
        out[plane] = turned.reshape(out.shape[1:]).astype(BF)

    def field_copy(sems, send, slab):
        def make(slot):
            target = partner(slot)
            return remote(
                send.at[:, target], slab.at[me],
                sems.at[0], sems.at[1], {"brick": target},
            )

        return make

    grad_copy = field_copy(grad_sems, grad_send, grad_slab)
    mixed_copy = field_copy(mixed_sems, mixed_send, mixed_slab)

    for plane in range(planes + 2):
        place(sums[1, plane], grad_send, plane)
    run_all(0, bricks - 1, grad_copy)
    grad_slab[me] = grad_send[:, me]

    tables[2].wait()
    lane = lax.broadcasted_iota(jnp.int32, (channels, LANES), 1) // channels
    for dx in range(3):
        for dy in range(3):
            tiled = []
            for dz in range(3):
                tap = taps_ref[9 * dx + 3 * dy + dz].astype(F32)
                tiled.append(jnp.concatenate([tap] * NZ, axis=1))
            lines = []
            for z in range(NZ):
                line = jnp.zeros((channels, LANES), F32)
                for dz in range(3):
                    line = jnp.where(lane == z - (dz - 1), tiled[dz], line)
                lines.append(line)
            square = jnp.concatenate(lines, axis=0)
            band[dx, dy * LANES : (dy + 1) * LANES, :] = square.astype(BF)
            back_band[2 - dx, (2 - dy) * LANES : (3 - dy) * LANES, :] = jnp.transpose(
                square, (1, 0)
            ).astype(BF)

    for way in range(2):
        edge_copy(way).wait()
    for plane in range(planes + 2):
        value = sums[0, plane]
        if plane < 2:
            value = value + low[plane].astype(F32)
        if plane >= planes:
            value = value + high[plane - planes].astype(F32)
        rounded = value.astype(BF)
        state[plane] = rounded
        cat[plane] = widen(rounded.astype(F32))
    for plane in range(planes):
        value = state[plane + 1].astype(F32)
        for dx in range(3):
            value = value + contract(cat[plane + dx], band[dx], (1, 0))
        place(value, mixed_send, plane)

    run_all(0, bricks - 1, mixed_copy)
    mixed_slab[me] = mixed_send[:, me]

    for load in tables[3:]:
        load.wait()
    rows = rows_ref[...]
    cols = (cols_ref[0], cols_ref[1])
    inv_cols = (inv_cols_ref[0], inv_cols_ref[1])
    inv_rows = (inv_rows_ref[0], inv_rows_ref[1])

    def transform(channel):
        tall = jnp.concatenate([field_f[:, z * per + channel, :] for z in range(NZ)], axis=0)
        tall = tall.astype(BF)
        first = contract(jnp.concatenate([tall, tall], axis=1), rows, (1, 0))
        halves = []
        for half in range(2):
            halves.append(
                jnp.concatenate(
                    [
                        first[z * NX : (z + 1) * NX, half * NY : (half + 1) * NY]
                        for z in range(NZ)
                    ],
                    axis=1,
                )
            )
        return three(cols, split(jnp.concatenate(halves, axis=0)))

    wait_for(grad_send.at[:, others], grad_slab.at[others], (grad_sems.at[0], grad_sems.at[1]))
    for brick in range(bricks):
        field = grad_slab[brick].astype(F32)
        before = grad_slab[(brick + bricks - 1) % bricks, planes + 1].astype(F32)
        after = grad_slab[(brick + 1) % bricks, 0].astype(F32)
        field_f[pl.ds(brick * planes, planes)] = field[1 : planes + 1]
        field_f[brick * planes] = field[1] + before
        field_f[(brick + 1) * planes - 1] = field[planes] + after
    wait_for(gain_slab.at[:, others], gain_slab.at[:, others], (gain_sems.at[0], gain_sems.at[1]))
    for channel in range(per):
        spectra[channel] = transform(channel)
        gain = jnp.transpose(gain_slab[channel].astype(F32).reshape(NY, NX), (1, 0))
        gain = jnp.concatenate([gain] * NZ, axis=1)
        gain = jnp.concatenate([gain, gain], axis=0)
        back = three(inv_cols, split(spectra[channel] * gain))
        flats = []
        for z in range(NZ):
            piece = back[:, z * NY : (z + 1) * NY]
            flats.append(jnp.concatenate([piece[:NX], piece[NX:]], axis=1))
        out = three(split(jnp.concatenate(flats, axis=0)), inv_rows) * (1.0 / (NX * NY))
        for z in range(NZ):
            back_f[:, z * per + channel, :] = out[z * NX : (z + 1) * NX]
    ext[pl.ds(2, NX)] = back_f[...].astype(BF)
    ext[pl.ds(0, 2)] = back_f[pl.ds(NX - 2, 2)].astype(BF)
    ext[pl.ds(NX + 2, 2)] = back_f[pl.ds(0, 2)].astype(BF)

    def ret_copy(slot):
        target = partner(slot)
        return remote(
            ext.at[pl.ds(target * planes, planes + 4)], ret.at[:, me],
            ret_sems.at[0], ret_sems.at[1], {"brick": target},
        )

    run_all(0, bricks - 1, ret_copy)
    ret[:, me] = ext[pl.ds(me * planes, planes + 4)]

    wait_for(mixed_send.at[:, others], mixed_slab.at[others], (mixed_sems.at[0], mixed_sems.at[1]))
    field_f[...] = mixed_slab[...].reshape(field_f.shape).astype(F32)
    scale = 1.0 / (NX * NY * math.sqrt(snaps * NZ))
    for channel in range(per):
        product = spectra[channel] * transform(channel)
        product = product[:NX] + product[NX:]
        part = product[:, :NY]
        for z in range(1, NZ):
            part = part + product[:, z * NY : (z + 1) * NY]
        part = jnp.transpose(part * scale, (1, 0))
        gain_send[channel] = part.reshape(gain_send.shape[1:]).astype(gain_send.dtype)

    def sibling(src, dst, sems):
        return remote(src, dst, sems.at[0], sems.at[1], {"snap": snaps - 1 - side})

    gain_swap = sibling(gain_send.at[1 - side], gain_pair, pair_sems.at[0])
    gain_swap.start()
    gain_swap.wait()
    gain_both[...] = (gain_send[side] + gain_pair[...]).astype(BF)

    def part_copy(step):
        other, device = device_of(step)
        return remote(
            gain_both.at[lax.rem(other, bricks)], gain_land.at[me * per + side],
            part_sems.at[0], part_sems.at[1], device,
        )

    run_all(1, total, part_copy)
    gain_land[me * per + side] = gain_both[me]

    wait_for(ret.at[:, others], ret.at[:, others], (ret_sems.at[0], ret_sems.at[1]))
    for plane in range(planes + 4):
        field = ret[plane].astype(F32).reshape(LANES, NY).astype(BF)
        back_cat[plane] = widen(contract(field, order, (0, 0)))
    own = back_cat[pl.ds(2, planes)].reshape(planes * NY, 3 * LANES)
    groups = [jnp.zeros((channels, LANES), F32) for _ in range(kernel_all.shape[0] * ROWS // channels)]
    tap_scale = 1.0 / math.sqrt(snaps * NX * NY * NZ)
    for dx in range(3):
        near = state[pl.ds(dx, planes)].reshape(planes * NY, LANES)
        gram = contract(near, own, (0, 0))
        for dy in range(3):
            square = gram[:, (2 - dy) * LANES : (3 - dy) * LANES]
            for dz in range(3):
                line = jnp.zeros((channels, LANES), F32)
                for z in range(NZ):
                    source = z + dz - 1
                    if 0 <= source < NZ:
                        line = jnp.where(
                            lane == z, square[source * channels : (source + 1) * channels], line
                        )
                line = line + pltpu.roll(line, LANES // 2, 1)
                line = line + pltpu.roll(line, LANES // 4, 1)
                tap = 9 * dx + 3 * dy + dz
                groups[tap // NZ] = jnp.where(
                    lane == tap % NZ, line * tap_scale, groups[tap // NZ]
                )
    tiles = channels // ROWS
    for position, value in enumerate(groups):
        kernel_part[position * tiles : (position + 1) * tiles] = value.reshape(tiles, ROWS, LANES)

    tap_swap = sibling(
        kernel_part.at[pl.ds((1 - side) * bricks, bricks)], kernel_pair, pair_sems.at[1]
    )
    tap_swap.start()

    def scatter(slot):
        target = partner(slot)
        return remote(
            kernel_both.at[target], kernel_land.at[me],
            red_sems.at[0, 0], red_sems.at[0, 1], {"brick": target},
        )

    def share(step):
        _, device = device_of(step)
        return remote(
            kernel_mine, kernel_all.at[flat], red_sems.at[1, 0], red_sems.at[1, 1], device,
        )

    for plane in range(planes + 2):
        value = back_cat[plane + 1, :, LANES : 2 * LANES].astype(F32)
        for dx in range(3):
            value = value + contract(back_cat[plane + dx], back_band[dx], (1, 0))
        pulled[plane] = value.astype(BF).astype(F32)
    for plane in range(planes + 2, PADX):
        pulled[plane] = jnp.zeros((NY, LANES), F32)

    tap_swap.wait()
    kernel_both[...] = kernel_part[pl.ds(side * bricks, bricks)] + kernel_pair[...]
    run_all(0, bricks - 1, scatter)
    kernel_land[me] = kernel_both[me]

    def gather_step(step, carry):
        here = pl.ds(pl.multiple_of(step * ROWS, ROWS), ROWS)
        turned = jnp.transpose(pulled[:, here, :], (1, 0, 2))
        for q in range(ROWS):
            y = step * ROWS + q
            lanes = pl.ds(pl.multiple_of(y * LANES, LANES), LANES)
            plane = turned[q]
            tall = jnp.concatenate(
                [plane[:, z * channels : (z + 1) * channels] for z in range(NZ)], axis=0
            )
            atom_ref[:, lanes] = contract(tall.astype(BF), blocks[y], (0, 0)).astype(BF)
        return carry

    steps = NY // ROWS
    lax.fori_loop(0, steps // 2, gather_step, 0)

    wait_for(kernel_land.at[others], kernel_land.at[others], (red_sems.at[0, 0], red_sems.at[0, 1]))
    kernel_mine[...] = jnp.sum(kernel_land[...], axis=0).astype(BF)
    run_all(1, total, share)
    kernel_all[flat] = kernel_mine[...]

    lax.fori_loop(steps // 2, steps, gather_step, 0)

    rest = pl.ds(0, total - 1)
    wait_for(gain_land.at[rest], gain_land.at[rest], (part_sems.at[0], part_sems.at[1]))
    gain_out_ref[...] = gain_land[...].astype(F32)
    wait_for(kernel_all.at[rest], kernel_all.at[rest], (red_sems.at[1, 0], red_sems.at[1, 1]))
    final = kernel_all[...].astype(F32).reshape(kernel_all.shape[0] * ROWS // channels, channels, LANES)
    for tap in range(kernel_ref.shape[0]):
        at = (tap % NZ) * channels
        kernel_ref[tap] = final[tap // NZ][:, at : at + channels]


def fast_shards(sizes, atom_features, cotangent, cell_index, assign_weight, conv_kernel, spectral_gain):
    snaps, bricks = sizes
    channels, atoms = atom_features.shape[1:]
    planes = NX // bricks
    per = channels // bricks
    group = NZ * per
    total = bricks * snaps
    chunks = 4
    order = np.zeros((LANES, LANES), np.float32)
    for brick in range(bricks):
        for z in range(NZ):
            for c in range(per):
                order[brick * group + z * per + c, z * channels + brick * per + c] = 1.0

    def angles(length):
        phase = np.outer(np.arange(length), np.arange(length)) % length
        turn = 2.0 * np.pi * phase / length
        return np.cos(turn), np.sin(turn)

    def halves(table):
        table = np.asarray(table, np.float32)
        high = table.astype(BF)
        low = (table - high.astype(np.float32)).astype(BF)
        return high, low

    col_cos, col_sin = angles(NX)
    row_cos, row_sin = angles(NY)
    rows = jnp.asarray(np.concatenate(halves(np.concatenate([row_cos, -row_sin], axis=1)), axis=0))
    cols = jnp.asarray(np.stack(halves(np.block([[col_cos, col_sin], [-col_sin, col_cos]]))))
    inv_cols = jnp.asarray(np.stack(halves(np.block([[col_cos, -col_sin], [col_sin, col_cos]]))))
    inv_rows = jnp.asarray(np.stack(halves(np.concatenate([row_cos, -row_sin], axis=0))))
    mesh_plane = (NY, LANES)
    send = (planes, bricks, group, NY)
    slab = (NX, group, NY)
    piece = (bricks, NY // bricks, NX)
    scratch = [
        ((channels, atoms), BF),
        ((channels, atoms), BF),
        ((CORNERS, atoms), jnp.int32),
        ((CORNERS, atoms), F32),
        (conv_kernel.shape, BF),
        ((channels,) + piece[1:], F32),
        (order.shape, BF),
        (rows.shape, BF),
        (cols.shape, BF),
        (inv_cols.shape, BF),
        (inv_rows.shape, BF),
        ((NY, NZ * PADX, LANES), BF),
        ((2, planes + 2) + mesh_plane, F32),
        ((4,) + mesh_plane, BF),
        ((2,) + mesh_plane, BF),
        ((2,) + mesh_plane, BF),
        ((3, 3 * LANES, LANES), BF),
        ((3, 3 * LANES, LANES), BF),
        ((planes + 2,) + mesh_plane, BF),
        ((planes + 2, NY, 3 * LANES), BF),
        ((planes + 2,) + send[1:], BF),
        (send, BF),
        ((bricks, planes + 2) + slab[1:], BF),
        ((bricks, planes) + slab[1:], BF),
        ((per,) + piece, BF),
        (slab, F32),
        (slab, F32),
        ((per, 2 * NX, NZ * NY), F32),
        ((NX + 4, group, NY), BF),
        ((planes + 4, bricks, group, NY), BF),
        ((planes + 4, NY, 3 * LANES), BF),
        ((PADX,) + mesh_plane, F32),
        ((channels,) + piece[1:], BF),
        ((per,) + piece, F32),
        (piece, F32),
        (piece, BF),
        ((channels,) + piece[1:], BF),
        ((total, ROWS, LANES), F32),
        ((bricks, ROWS, LANES), F32),
        ((bricks, ROWS, LANES), F32),
        ((bricks, ROWS, LANES), F32),
        ((ROWS, LANES), BF),
        ((total, ROWS, LANES), BF),
    ]
    sems = [(2, 2)] + [(2,)] * 5 + [(2, 2)] * 2 + [(4, chunks), (7,)]
    atom_grad, kernel_grad, gain_grad = pl.pallas_call(
        lambda *refs: whole_body(bricks, snaps, chunks, *refs),
        out_shape=[
            pltpu.VMEM((channels, atoms), BF),
            pltpu.VMEM(conv_kernel.shape, F32),
            pltpu.VMEM((channels,) + piece[1:], F32),
        ],
        in_specs=[pl.BlockSpec(memory_space=pl.ANY)] * 11,
        out_specs=[vmem()] * 3,
        scratch_shapes=[pltpu.VMEM(dims, kind) for dims, kind in scratch]
        + [pltpu.SemaphoreType.DMA(dims) for dims in sems],
        compiler_params=pltpu.CompilerParams(
            collective_id=1, has_side_effects=True, vmem_limit_bytes=60 * 1024 * 1024
        ),
    )(
        atom_features[0], cotangent[0], cell_index[0], assign_weight[0], conv_kernel,
        jnp.transpose(spectral_gain, (0, 2, 1)), jnp.asarray(order, BF), rows, cols,
        inv_cols, inv_rows,
    )
    return (atom_grad[None], kernel_grad, jnp.transpose(gain_grad, (0, 2, 1)))


def fits(mesh, channels, atoms):
    bricks = mesh.shape["brick"]
    snaps = mesh.shape["snap"]
    return (
        channels * NZ == LANES
        and NX == LANES
        and NY == LANES
        and atoms // bricks == NY * LANES
        and channels % bricks == 0
        and snaps == 2
        and NZ * channels // bricks == ROWS
        and NX // bricks == ROWS
        and 8 * channels == bricks * snaps * ROWS
    )


def solution(mesh):
    placed = (
        P("snap", None, "brick"),
        P("snap", None, "brick"),
        P("snap", None, "brick"),
        P("snap", None, "brick"),
        P(),
        P(None, None, "brick"),
    )
    sizes = (mesh.shape["snap"], mesh.shape["brick"])

    def pick(*arguments):
        if fits(mesh, arguments[0].shape[1], arguments[0].shape[2] * sizes[1]):
            return fast_shards(sizes, *arguments)
        return shards(*arguments)

    return jax.shard_map(
        pick,
        mesh=mesh,
        in_specs=placed,
        out_specs=(P("snap", None, "brick"), P(), P(None, None, "brick")),
        check_vma=False,
    )
```

```python
import math

import jax
import jax.numpy as jnp
from jax import lax
import numpy as np
from jax.experimental import pallas as pl
from jax.experimental.pallas import tpu as pltpu
from jax.sharding import PartitionSpec as P

NX = 128
NY = 128
NZ = 4
CORNERS = 4


HIGHEST = lax.Precision.HIGHEST


def from_behind(value, axis, steps):
    count = lax.axis_size(axis)
    pairs = [(source, (source + steps) % count) for source in range(count)]
    return lax.ppermute(value, axis, pairs)


def with_halo(cells, sides, width):
    for axis, dim in sides:
        count = lax.axis_size(axis)
        head = lax.slice_in_dim(cells, 0, width, axis=dim)
        tail = lax.slice_in_dim(cells, cells.shape[dim] - width, cells.shape[dim], axis=dim)
        cells = jnp.concatenate(
            [
                lax.ppermute(tail, axis, [(i, (i + 1) % count) for i in range(count)]),
                cells,
                lax.ppermute(head, axis, [((i + 1) % count, i) for i in range(count)]),
            ],
            axis=dim,
        )
    return cells


def tables(length):
    indices = jnp.arange(length, dtype=jnp.int32)
    phases = indices[:, None] * indices[None, :] % length
    angles = phases.astype(jnp.float32) * (2.0 * math.pi / length)
    return (jnp.cos(angles), jnp.sin(angles))


def patches(padded, first_plane, planes):
    row_total = padded.shape[1]
    thickness = padded.shape[3]
    wrapped = jnp.concatenate([padded[:, -1:], padded, padded[:, :1]], axis=1)
    widened = jnp.pad(wrapped, ((0, 0), (0, 0), (0, 0), (1, 1)))
    pieces = []
    for step_first in (-1, 0, 1):
        for step_second in (-1, 0, 1):
            for step_third in (-1, 0, 1):
                pieces.append(
                    widened[
                        :,
                        1 + step_second : 1 + step_second + row_total,
                        first_plane + step_first : first_plane + step_first + planes,
                        1 + step_third : 1 + step_third + thickness,
                    ]
                )
    return jnp.stack(pieces)


def transform_rows(mesh_field, row_cosine, row_sine):
    real_part = jnp.einsum("cyxz,yk->ckxz", mesh_field, row_cosine, precision=HIGHEST)
    imag_part = -jnp.einsum("cyxz,yk->ckxz", mesh_field, row_sine, precision=HIGHEST)
    return jnp.stack([real_part, imag_part])


def transform_columns(stacked, col_cosine, col_sine, sign_value):

    def apply_table(part_values, table):
        return jnp.einsum("ckxz,xq->ckqz", part_values, table, precision=HIGHEST)

    real_part = stacked[0]
    imag_part = stacked[1]
    new_real = apply_table(real_part, col_cosine) + sign_value * apply_table(imag_part, col_sine)
    new_imag = apply_table(imag_part, col_cosine) - sign_value * apply_table(real_part, col_sine)
    return jnp.stack([new_real, new_imag])


def shards(atom_features, cotangent, cell_index, assign_weight, conv_kernel, spectral_gain):
    channels = atom_features.shape[1]
    slot_count = atom_features.shape[2] // NY
    own_planes = NX // lax.axis_size("brick")
    tile_cells = (own_planes + 2) * NZ
    snap_count = lax.axis_size("snap")
    index_tiles = cell_index[0].reshape(CORNERS, NY, slot_count)
    weight_tiles = assign_weight[0].astype(jnp.bfloat16).reshape(CORNERS, NY, slot_count)
    cell_numbers = jnp.arange(tile_cells, dtype=jnp.int32)
    blocks = jnp.zeros((NY, tile_cells, slot_count), jnp.bfloat16)
    for corner in range(CORNERS):
        matches = index_tiles[corner][:, None, :] == cell_numbers[None, :, None]
        blocks = blocks + jnp.where(
            matches, weight_tiles[corner][:, None, :], jnp.zeros((), jnp.bfloat16)
        )
    stacked = jnp.concatenate([atom_features[0], cotangent[0]], axis=0).reshape(
        2 * channels, NY, slot_count
    )
    spread = jnp.einsum("cts,tjs->ctj", stacked, blocks, preferred_element_type=jnp.float32)
    spread = spread.reshape(2 * channels, NY, own_planes + 2, NZ)
    from_above = from_behind(spread[:, :, 0], "brick", -1)
    from_below = from_behind(spread[:, :, own_planes + 1], "brick", 1)
    owned_planes = spread[:, :, 1 : own_planes + 1]
    owned_planes = owned_planes.at[:, :, 0].add(from_below)
    owned_planes = owned_planes.at[:, :, own_planes - 1].add(from_above)
    state_bf = owned_planes[:channels].astype(jnp.bfloat16)
    grad_mesh = owned_planes[channels:]
    col_cosine, col_sine = tables(NX)
    row_cosine, row_sine = tables(NY)

    def make_rows(mesh_field):
        return transform_rows(mesh_field, row_cosine, row_sine)

    def to_columns(part_rows):
        return transform_columns(part_rows, col_cosine, col_sine, 1.0)

    grad_rows = make_rows(grad_mesh)
    grad_spec = to_columns(
        lax.all_to_all(grad_rows, "brick", split_axis=2, concat_axis=3, tiled=True)
    )
    state_rim = with_halo(state_bf, (("brick", 2),), 1)
    state_patch = patches(state_rim, 1, own_planes)
    conv_out = jnp.einsum(
        "tcyxz,tcd->dyxz", state_patch, conv_kernel, preferred_element_type=jnp.float32
    )
    mesh_mixed = state_bf.astype(jnp.float32) + conv_out
    mixed_rows = make_rows(mesh_mixed)
    state_spec = to_columns(
        lax.all_to_all(
            mixed_rows.astype(jnp.bfloat16), "brick", split_axis=2, concat_axis=3, tiled=True
        ).astype(mixed_rows.dtype)
    )
    products = jnp.sum(grad_spec[0] * state_spec[0] + grad_spec[1] * state_spec[1], axis=3)
    gain_part = jnp.transpose(products, (0, 2, 1)) / (NX * NY * math.sqrt(snap_count * NZ))
    gain_local = jnp.transpose(spectral_gain, (0, 2, 1))
    filtered = grad_spec * gain_local[None, :, :, :, None]
    before_cross = transform_columns(filtered, col_cosine, col_sine, -1.0)
    part_cols = lax.all_to_all(before_cross, "brick", split_axis=3, concat_axis=2, tiled=True)
    real_rows = jnp.einsum("ckxz,ky->cyxz", part_cols[0], row_cosine, precision=HIGHEST)
    imag_rows = jnp.einsum("ckxz,ky->cyxz", part_cols[1], row_sine, precision=HIGHEST)
    grad_mixed = (real_rows - imag_rows) / (NX * NY)
    grad_bf = grad_mixed.astype(jnp.bfloat16)
    flipped = conv_kernel[::-1]
    grad_padded = with_halo(grad_bf, (("brick", 2),), 1)
    grad_patch = patches(grad_padded, 1, own_planes)
    back_conv = jnp.einsum(
        "tdyxz,tcd->cyxz", grad_patch, flipped, preferred_element_type=jnp.float32
    )
    pulled = (grad_bf.astype(jnp.float32) + back_conv).astype(jnp.bfloat16)
    pulled_full = with_halo(pulled, (("brick", 2),), 1)
    kernel_part = jnp.einsum(
        "tcyxz,dyxz->tcd", state_patch, grad_bf, preferred_element_type=jnp.float32
    )
    kernel_part = kernel_part / math.sqrt(snap_count * NX * NY * NZ)
    pulled_tiles = pulled_full.reshape(channels, NY, tile_cells)
    atom_total = jnp.einsum(
        "ctj,tjs->cts", pulled_tiles, blocks, preferred_element_type=jnp.float32
    )
    atom_grad = atom_total.astype(jnp.bfloat16).reshape(1, channels, NY * slot_count)
    kernel_grad = lax.psum(kernel_part, ("snap", "brick"))
    gain_grad = lax.psum(gain_part, "snap")
    return (atom_grad, kernel_grad, gain_grad)


BF = jnp.bfloat16
F32 = jnp.float32
LANES = 128
ROWS = 8
PADX = 16
MESH = pl.DeviceIdType.MESH


def contract(left, right, dims, precision=None):
    return lax.dot_general(
        left, right, ((dims[:1], dims[1:]), ((), ())),
        precision=precision, preferred_element_type=F32,
    )


def vmem():
    return pl.BlockSpec(memory_space=pltpu.VMEM)


def shape_of(dims, kind):
    return jax.ShapeDtypeStruct(dims, kind)


def corner_block(index_ref, weight_ref, lanes, cell_of_row):
    block = jnp.zeros(cell_of_row.shape, F32)
    index = index_ref[:, lanes]
    weight = weight_ref[:, lanes]
    for corner in range(CORNERS):
        block = jnp.where(
            index[corner : corner + 1] == cell_of_row, weight[corner : corner + 1], block
        )
    return block.astype(BF)


def row_cells():
    row = lax.broadcasted_iota(jnp.int32, (NZ * PADX, LANES), 0)
    return (row % PADX) * NZ + row // PADX


def run_all(first, total, make):
    def go(step, carry):
        make(step).start()
        return carry

    lax.fori_loop(first, total, go, 0)


def wait_all(first, total, make):
    def finish(step, carry):
        make(step).wait()
        return carry

    lax.fori_loop(first, total, finish, 0)


def split(value):
    high = value.astype(BF)
    return high, (value - high.astype(F32)).astype(BF)


def three(left, right):
    left_high, left_low = left
    right_high, right_low = right
    return (
        contract(left_high, right_high, (1, 0))
        + contract(left_high, right_low, (1, 0))
        + contract(left_low, right_high, (1, 0))
    )


def widen(value):
    return jnp.concatenate(
        [jnp.roll(value, 1, axis=0), value, jnp.roll(value, -1, axis=0)], axis=1
    ).astype(BF)


def whole_body(
    bricks, snaps, chunks,
    feature_hbm, cotangent_hbm, index_hbm, weight_hbm, taps_hbm, gain_hbm,
    order_hbm, rows_hbm, cols_hbm, inv_cols_hbm, inv_rows_hbm,
    atom_ref, kernel_ref, gain_out_ref,
    feature_ref, cotangent_ref, index_ref, weight_ref, taps_ref, gain_ref,
    order_ref, rows_ref, cols_ref, inv_cols_ref, inv_rows_ref,
    blocks, sums, edge, low, high, band, back_band, state, cat, grad_send, mixed_send,
    grad_slab, mixed_slab, gain_slab, field_f, back_f, spectra, ext, ret, back_cat, pulled,
    gain_out, gain_send, gain_pair, gain_both, part_all,
    kernel_part, kernel_land, kernel_mine, kernel_all,
    edge_sems, grad_sems, mixed_sems, gain_sems, ret_sems, part_sems, pair_sems, red_sems,
    in_sem, table_sem,
):
    channels = feature_ref.shape[0]
    planes = NX // bricks
    per = channels // bricks
    total = bricks * snaps
    me = lax.axis_index("brick")
    side = lax.axis_index("snap")
    flat = side * bricks + me
    above = lax.rem(me + 1, bricks)
    below = lax.rem(me + bricks - 1, bricks)
    barrier = pltpu.get_barrier_semaphore()

    def device_of(step):
        other = lax.rem(flat + step, total)
        return other, {"snap": other // bricks, "brick": lax.rem(other, bricks)}

    def hello(step, carry):
        pl.semaphore_signal(barrier, inc=1, device_id=device_of(step)[1], device_id_type=MESH)
        return carry

    def remote(src, dst, send_sem, recv_sem, device):
        return pltpu.make_async_remote_copy(
            src_ref=src, dst_ref=dst, send_sem=send_sem, recv_sem=recv_sem,
            device_id=device, device_id_type=MESH,
        )

    def partner(slot):
        return lax.rem(me + 1 + slot, bricks)

    def wait_for(src, dst, sems):
        remote(src, dst, sems[0], sems[1], {"brick": above}).wait()

    others = pl.ds(0, bricks - 1)
    span = NY // chunks
    tables = [
        pltpu.make_async_copy(src, dst, table_sem.at[number])
        for number, (src, dst) in enumerate(
            [
                (gain_hbm, gain_ref), (order_hbm, order_ref), (taps_hbm, taps_ref),
                (rows_hbm, rows_ref), (cols_hbm, cols_ref), (inv_cols_hbm, inv_cols_ref),
                (inv_rows_hbm, inv_rows_ref),
            ]
        )
    ]
    loads = []
    for chunk in range(chunks):
        lanes = pl.ds(chunk * span * LANES, span * LANES)
        loads.append(
            [
                pltpu.make_async_copy(src.at[:, lanes], dst.at[:, lanes], in_sem.at[number, chunk])
                for number, (src, dst) in enumerate(
                    [
                        (index_hbm, index_ref), (weight_hbm, weight_ref),
                        (feature_hbm, feature_ref), (cotangent_hbm, cotangent_ref),
                    ]
                )
            ]
        )
    for load in loads[0]:
        load.start()
    lax.fori_loop(1, total, hello, 0)
    for load in loads[1]:
        load.start()

    cells = row_cells()

    def spread_step(step, carry):
        parts = [[], []]
        for q in range(ROWS):
            y = step * ROWS + q
            lanes = pl.ds(pl.multiple_of(y * LANES, LANES), LANES)
            block = corner_block(index_ref, weight_ref, lanes, cells)
            blocks[y] = block
            stacked = jnp.concatenate([feature_ref[:, lanes], cotangent_ref[:, lanes]], axis=0)
            found = contract(block, stacked, (1, 1))
            for f in range(2):
                parts[f].append(
                    jnp.concatenate(
                        [
                            found[z * PADX : (z + 1) * PADX, f * channels : (f + 1) * channels]
                            for z in range(NZ)
                        ],
                        axis=1,
                    )
                )
        for f in range(2):
            turned = jnp.transpose(jnp.stack(parts[f]), (1, 0, 2))
            sums[f, :, pl.ds(pl.multiple_of(step * ROWS, ROWS), ROWS), :] = turned[: planes + 2]
        return carry

    def gain_copy(slot):
        target = partner(slot)
        return remote(
            gain_out.at[pl.ds(target * per, per)], gain_slab.at[:, me],
            gain_sems.at[0], gain_sems.at[1], {"brick": target},
        )

    def edge_copy(way):
        return remote(
            edge.at[pl.ds(2 * way, 2)], low if way == 0 else high,
            edge_sems.at[way, 0], edge_sems.at[way, 1], {"brick": above if way == 0 else below},
        )

    for chunk in range(chunks):
        for load in loads[chunk]:
            load.wait()
        if chunk + 2 < chunks:
            for load in loads[chunk + 2]:
                load.start()
        if chunk + 2 == chunks:
            for load in tables:
                load.start()
        if chunk == chunks - 1:
            tables[0].wait()
            gain_out[...] = gain_ref[...].astype(BF)
            gain_slab[:, me] = gain_out[pl.ds(me * per, per)]
            pl.semaphore_wait(barrier, total - 1)
            run_all(0, bricks - 1, gain_copy)
        lax.fori_loop(chunk * (span // ROWS), (chunk + 1) * (span // ROWS), spread_step, 0)
    for slot, plane in enumerate([planes, planes + 1, 0, 1]):
        edge[slot] = sums[0, plane].astype(BF)

    for way in range(2):
        edge_copy(way).start()
    tables[1].wait()
    order = order_ref[...]

    def place(field, out, plane):
        turned = contract(order, field.astype(BF), (1, 1))
        out[plane] = turned.reshape(out.shape[1:]).astype(BF)

    def field_copy(sems, send, slab):
        def make(slot):
            target = partner(slot)
            return remote(
                send.at[:, target], slab.at[me],
                sems.at[0], sems.at[1], {"brick": target},
            )

        return make

    grad_copy = field_copy(grad_sems, grad_send, grad_slab)
    def mixed_copy(first, count):
        some = pl.ds(first, count)

        def make(slot):
            target = partner(slot)
            return remote(
                mixed_send.at[some, target], mixed_slab.at[me, some],
                mixed_sems.at[0], mixed_sems.at[1], {"brick": target},
            )

        return make


    for plane in range(planes + 2):
        place(sums[1, plane], grad_send, plane)
    run_all(0, bricks - 1, grad_copy)
    grad_slab[me] = grad_send[:, me]

    tables[2].wait()
    lane = lax.broadcasted_iota(jnp.int32, (channels, LANES), 1) // channels
    for dx in range(3):
        for dy in range(3):
            tiled = []
            for dz in range(3):
                tap = taps_ref[9 * dx + 3 * dy + dz].astype(F32)
                tiled.append(jnp.concatenate([tap] * NZ, axis=1))
            lines = []
            for z in range(NZ):
                line = jnp.zeros((channels, LANES), F32)
                for dz in range(3):
                    line = jnp.where(lane == z - (dz - 1), tiled[dz], line)
                lines.append(line)
            square = jnp.concatenate(lines, axis=0)
            band[dx, dy * LANES : (dy + 1) * LANES, :] = square.astype(BF)
            back_band[2 - dx, (2 - dy) * LANES : (3 - dy) * LANES, :] = jnp.transpose(
                square, (1, 0)
            ).astype(BF)

    def settle(plane, value):
        rounded = value.astype(BF)
        state[plane] = rounded
        cat[plane] = widen(rounded.astype(F32))

    def convolve(plane):
        value = state[plane + 1].astype(F32)
        for dx in range(3):
            value = value + contract(cat[plane + dx], band[dx], (1, 0))
        place(value, mixed_send, plane)

    for plane in range(2, planes):
        settle(plane, sums[0, plane])
    for plane in range(2, planes - 2):
        convolve(plane)
    run_all(0, bricks - 1, mixed_copy(2, planes - 4))
    for way in range(2):
        edge_copy(way).wait()
    for plane in range(2):
        settle(plane, sums[0, plane] + low[plane].astype(F32))
        settle(planes + plane, sums[0, planes + plane] + high[plane].astype(F32))
    for plane in (0, 1, planes - 2, planes - 1):
        convolve(plane)
    run_all(0, bricks - 1, mixed_copy(0, 2))
    run_all(0, bricks - 1, mixed_copy(planes - 2, 2))
    mixed_slab[me] = mixed_send[:, me]

    for load in tables[3:]:
        load.wait()
    rows = rows_ref[...]
    cols = (cols_ref[0], cols_ref[1])
    inv_cols = (inv_cols_ref[0], inv_cols_ref[1])
    inv_rows = (inv_rows_ref[0], inv_rows_ref[1])

    def transform(channel):
        tall = jnp.concatenate([field_f[:, z * per + channel, :] for z in range(NZ)], axis=0)
        tall = tall.astype(BF)
        first = contract(jnp.concatenate([tall, tall], axis=1), rows, (1, 0))
        halves = []
        for half in range(2):
            halves.append(
                jnp.concatenate(
                    [
                        first[z * NX : (z + 1) * NX, half * NY : (half + 1) * NY]
                        for z in range(NZ)
                    ],
                    axis=1,
                )
            )
        return three(cols, split(jnp.concatenate(halves, axis=0)))

    wait_for(grad_send.at[:, others], grad_slab.at[others], (grad_sems.at[0], grad_sems.at[1]))
    for brick in range(bricks):
        field = grad_slab[brick].astype(F32)
        before = grad_slab[(brick + bricks - 1) % bricks, planes + 1].astype(F32)
        after = grad_slab[(brick + 1) % bricks, 0].astype(F32)
        field_f[pl.ds(brick * planes, planes)] = field[1 : planes + 1]
        field_f[brick * planes] = field[1] + before
        field_f[(brick + 1) * planes - 1] = field[planes] + after
    wait_for(gain_slab.at[:, others], gain_slab.at[:, others], (gain_sems.at[0], gain_sems.at[1]))
    for channel in range(per):
        spectra[channel] = transform(channel)
        gain = jnp.transpose(gain_slab[channel].astype(F32).reshape(NY, NX), (1, 0))
        gain = jnp.concatenate([gain] * NZ, axis=1)
        gain = jnp.concatenate([gain, gain], axis=0)
        back = three(inv_cols, split(spectra[channel] * gain))
        flats = []
        for z in range(NZ):
            piece = back[:, z * NY : (z + 1) * NY]
            flats.append(jnp.concatenate([piece[:NX], piece[NX:]], axis=1))
        out = three(split(jnp.concatenate(flats, axis=0)), inv_rows) * (1.0 / (NX * NY))
        for z in range(NZ):
            back_f[:, z * per + channel, :] = out[z * NX : (z + 1) * NX]
    ext[pl.ds(2, NX)] = back_f[...].astype(BF)
    ext[pl.ds(0, 2)] = back_f[pl.ds(NX - 2, 2)].astype(BF)
    ext[pl.ds(NX + 2, 2)] = back_f[pl.ds(0, 2)].astype(BF)

    def ret_copy(slot):
        target = partner(slot)
        return remote(
            ext.at[pl.ds(target * planes, planes + 4)], ret.at[:, me],
            ret_sems.at[0], ret_sems.at[1], {"brick": target},
        )

    run_all(0, bricks - 1, ret_copy)
    ret[:, me] = ext[pl.ds(me * planes, planes + 4)]

    wait_for(mixed_send.at[:, others], mixed_slab.at[others], (mixed_sems.at[0], mixed_sems.at[1]))
    field_f[...] = mixed_slab[...].reshape(field_f.shape).astype(F32)
    scale = 1.0 / (NX * NY * math.sqrt(snaps * NZ))
    for channel in range(per):
        product = spectra[channel] * transform(channel)
        product = product[:NX] + product[NX:]
        part = product[:, :NY]
        for z in range(1, NZ):
            part = part + product[:, z * NY : (z + 1) * NY]
        part = jnp.transpose(part * scale, (1, 0))
        gain_send[channel] = part.reshape(gain_send.shape[1:]).astype(gain_send.dtype)

    def part_copy(step):
        other, device = device_of(step)
        return remote(
            gain_send.at[other // bricks, lax.rem(other, bricks)], part_all.at[flat],
            part_sems.at[0], part_sems.at[1], device,
        )

    wait_for(ret.at[:, others], ret.at[:, others], (ret_sems.at[0], ret_sems.at[1]))
    for plane in range(planes + 4):
        field = ret[plane].astype(F32).reshape(LANES, NY).astype(BF)
        back_cat[plane] = widen(contract(field, order, (0, 0)))
    own = back_cat[pl.ds(2, planes)].reshape(planes * NY, 3 * LANES)
    groups = [jnp.zeros((channels, LANES), F32) for _ in range(kernel_all.shape[0] * ROWS // channels)]
    tap_scale = 1.0 / math.sqrt(snaps * NX * NY * NZ)
    for dx in range(3):
        near = state[pl.ds(dx, planes)].reshape(planes * NY, LANES)
        gram = contract(near, own, (0, 0))
        for dy in range(3):
            square = gram[:, (2 - dy) * LANES : (3 - dy) * LANES]
            for dz in range(3):
                line = jnp.zeros((channels, LANES), F32)
                for z in range(NZ):
                    source = z + dz - 1
                    if 0 <= source < NZ:
                        line = jnp.where(
                            lane == z, square[source * channels : (source + 1) * channels], line
                        )
                line = line + pltpu.roll(line, LANES // 2, 1)
                line = line + pltpu.roll(line, LANES // 4, 1)
                tap = 9 * dx + 3 * dy + dz
                groups[tap // NZ] = jnp.where(
                    lane == tap % NZ, line * tap_scale, groups[tap // NZ]
                )
    tiles = channels // ROWS
    for position, value in enumerate(groups):
        kernel_part[position * tiles : (position + 1) * tiles] = value.reshape(
            tiles, ROWS, LANES
        ).astype(BF)

    def scatter(step):
        other, device = device_of(step)
        return remote(
            kernel_part.at[other], kernel_land.at[flat],
            red_sems.at[0, 0], red_sems.at[0, 1], device,
        )

    def share(step):
        _, device = device_of(step)
        return remote(
            kernel_mine, kernel_all.at[flat], red_sems.at[1, 0], red_sems.at[1, 1], device,
        )

    run_all(1, total, scatter)
    kernel_land[flat] = kernel_part[flat]
    run_all(1, total, part_copy)
    part_all[flat] = gain_send[side, me]
    rest = pl.ds(0, total - 1)

    for plane in range(planes + 2):
        value = back_cat[plane + 1, :, LANES : 2 * LANES].astype(F32)
        for dx in range(3):
            value = value + contract(back_cat[plane + dx], back_band[dx], (1, 0))
        pulled[plane] = value.astype(BF).astype(F32)
    for plane in range(planes + 2, PADX):
        pulled[plane] = jnp.zeros((NY, LANES), F32)

    def gather_step(step, carry):
        here = pl.ds(pl.multiple_of(step * ROWS, ROWS), ROWS)
        turned = jnp.transpose(pulled[:, here, :], (1, 0, 2))
        for q in range(ROWS):
            y = step * ROWS + q
            lanes = pl.ds(pl.multiple_of(y * LANES, LANES), LANES)
            plane = turned[q]
            tall = jnp.concatenate(
                [plane[:, z * channels : (z + 1) * channels] for z in range(NZ)], axis=0
            )
            atom_ref[:, lanes] = contract(tall.astype(BF), blocks[y], (0, 0)).astype(BF)
        return carry

    steps = NY // ROWS
    lax.fori_loop(0, steps // 2, gather_step, 0)

    wait_for(kernel_land.at[rest], kernel_land.at[rest], (red_sems.at[0, 0], red_sems.at[0, 1]))
    kernel_mine[...] = jnp.sum(kernel_land[...].astype(F32), axis=0).astype(BF)
    run_all(1, total, share)
    kernel_all[flat] = kernel_mine[...]

    wait_for(part_all.at[rest], part_all.at[rest], (part_sems.at[0], part_sems.at[1]))
    gain_both[...] = part_all[pl.ds(0, bricks)].astype(F32) + part_all[pl.ds(bricks, bricks)].astype(F32)
    gain_swap = remote(
        gain_both, gain_pair, pair_sems.at[0], pair_sems.at[1], {"snap": snaps - 1 - side}
    )
    gain_swap.start()

    lax.fori_loop(steps // 2, steps, gather_step, 0)

    gain_swap.wait()
    for brick in range(bricks):
        gain_out_ref[brick * per + side] = gain_both[brick]
        gain_out_ref[brick * per + 1 - side] = gain_pair[brick]
    wait_for(kernel_all.at[rest], kernel_all.at[rest], (red_sems.at[1, 0], red_sems.at[1, 1]))
    final = kernel_all[...].astype(F32).reshape(kernel_all.shape[0] * ROWS // channels, channels, LANES)
    for tap in range(kernel_ref.shape[0]):
        at = (tap % NZ) * channels
        kernel_ref[tap] = final[tap // NZ][:, at : at + channels]


def fast_shards(sizes, atom_features, cotangent, cell_index, assign_weight, conv_kernel, spectral_gain):
    snaps, bricks = sizes
    channels, atoms = atom_features.shape[1:]
    planes = NX // bricks
    per = channels // bricks
    group = NZ * per
    total = bricks * snaps
    chunks = 4
    order = np.zeros((LANES, LANES), np.float32)
    for brick in range(bricks):
        for z in range(NZ):
            for c in range(per):
                order[brick * group + z * per + c, z * channels + brick * per + c] = 1.0

    def angles(length):
        phase = np.outer(np.arange(length), np.arange(length)) % length
        turn = 2.0 * np.pi * phase / length
        return np.cos(turn), np.sin(turn)

    def halves(table):
        table = np.asarray(table, np.float32)
        high = table.astype(BF)
        low = (table - high.astype(np.float32)).astype(BF)
        return high, low

    col_cos, col_sin = angles(NX)
    row_cos, row_sin = angles(NY)
    rows = jnp.asarray(np.concatenate(halves(np.concatenate([row_cos, -row_sin], axis=1)), axis=0))
    cols = jnp.asarray(np.stack(halves(np.block([[col_cos, col_sin], [-col_sin, col_cos]]))))
    inv_cols = jnp.asarray(np.stack(halves(np.block([[col_cos, -col_sin], [col_sin, col_cos]]))))
    inv_rows = jnp.asarray(np.stack(halves(np.concatenate([row_cos, -row_sin], axis=0))))
    mesh_plane = (NY, LANES)
    send = (planes, bricks, group, NY)
    slab = (NX, group, NY)
    piece = (bricks, NY // bricks, NX)
    scratch = [
        ((channels, atoms), BF),
        ((channels, atoms), BF),
        ((CORNERS, atoms), jnp.int32),
        ((CORNERS, atoms), F32),
        (conv_kernel.shape, BF),
        ((channels,) + piece[1:], F32),
        (order.shape, BF),
        (rows.shape, BF),
        (cols.shape, BF),
        (inv_cols.shape, BF),
        (inv_rows.shape, BF),
        ((NY, NZ * PADX, LANES), BF),
        ((2, planes + 2) + mesh_plane, F32),
        ((4,) + mesh_plane, BF),
        ((2,) + mesh_plane, BF),
        ((2,) + mesh_plane, BF),
        ((3, 3 * LANES, LANES), BF),
        ((3, 3 * LANES, LANES), BF),
        ((planes + 2,) + mesh_plane, BF),
        ((planes + 2, NY, 3 * LANES), BF),
        ((planes + 2,) + send[1:], BF),
        (send, BF),
        ((bricks, planes + 2) + slab[1:], BF),
        ((bricks, planes) + slab[1:], BF),
        ((per,) + piece, BF),
        (slab, F32),
        (slab, F32),
        ((per, 2 * NX, NZ * NY), F32),
        ((NX + 4, group, NY), BF),
        ((planes + 4, bricks, group, NY), BF),
        ((planes + 4, NY, 3 * LANES), BF),
        ((PADX,) + mesh_plane, F32),
        ((channels,) + piece[1:], BF),
        ((per,) + piece, BF),
        (piece, F32),
        (piece, F32),
        ((total,) + piece[1:], BF),
        ((total, ROWS, LANES), BF),
        ((total, ROWS, LANES), BF),
        ((ROWS, LANES), BF),
        ((total, ROWS, LANES), BF),
    ]
    sems = [(2, 2)] + [(2,)] * 6 + [(2, 2)] + [(4, chunks), (7,)]
    atom_grad, kernel_grad, gain_grad = pl.pallas_call(
        lambda *refs: whole_body(bricks, snaps, chunks, *refs),
        out_shape=[
            pltpu.VMEM((channels, atoms), BF),
            pltpu.VMEM(conv_kernel.shape, F32),
            pltpu.VMEM((channels,) + piece[1:], F32),
        ],
        in_specs=[pl.BlockSpec(memory_space=pl.ANY)] * 11,
        out_specs=[vmem()] * 3,
        scratch_shapes=[pltpu.VMEM(dims, kind) for dims, kind in scratch]
        + [pltpu.SemaphoreType.DMA(dims) for dims in sems],
        compiler_params=pltpu.CompilerParams(
            collective_id=1, has_side_effects=True, vmem_limit_bytes=60 * 1024 * 1024
        ),
    )(
        atom_features[0], cotangent[0], cell_index[0], assign_weight[0], conv_kernel,
        jnp.transpose(spectral_gain, (0, 2, 1)), jnp.asarray(order, BF), rows, cols,
        inv_cols, inv_rows,
    )
    return (atom_grad[None], kernel_grad, jnp.transpose(gain_grad, (0, 2, 1)))


def fits(mesh, channels, atoms):
    bricks = mesh.shape["brick"]
    snaps = mesh.shape["snap"]
    return (
        channels * NZ == LANES
        and NX == LANES
        and NY == LANES
        and atoms // bricks == NY * LANES
        and channels % bricks == 0
        and snaps == 2
        and NZ * channels // bricks == ROWS
        and NX // bricks == ROWS
        and 8 * channels == bricks * snaps * ROWS
    )


def solution(mesh):
    placed = (
        P("snap", None, "brick"),
        P("snap", None, "brick"),
        P("snap", None, "brick"),
        P("snap", None, "brick"),
        P(),
        P(None, None, "brick"),
    )
    sizes = (mesh.shape["snap"], mesh.shape["brick"])

    def pick(*arguments):
        if fits(mesh, arguments[0].shape[1], arguments[0].shape[2] * sizes[1]):
            return fast_shards(sizes, *arguments)
        return shards(*arguments)

    return jax.shard_map(
        pick,
        mesh=mesh,
        in_specs=placed,
        out_specs=(P("snap", None, "brick"), P(), P(None, None, "brick")),
        check_vma=False,
    )
```

```python
import math

import jax
import jax.numpy as jnp
from jax import lax
import numpy as np
from jax.experimental import pallas as pl
from jax.experimental.pallas import tpu as pltpu
from jax.sharding import PartitionSpec as P

NX = 128
NY = 128
NZ = 4
CORNERS = 4


HIGHEST = lax.Precision.HIGHEST


def from_behind(value, axis, steps):
    count = lax.axis_size(axis)
    pairs = [(source, (source + steps) % count) for source in range(count)]
    return lax.ppermute(value, axis, pairs)


def with_halo(cells, sides, width):
    for axis, dim in sides:
        count = lax.axis_size(axis)
        head = lax.slice_in_dim(cells, 0, width, axis=dim)
        tail = lax.slice_in_dim(cells, cells.shape[dim] - width, cells.shape[dim], axis=dim)
        cells = jnp.concatenate(
            [
                lax.ppermute(tail, axis, [(i, (i + 1) % count) for i in range(count)]),
                cells,
                lax.ppermute(head, axis, [((i + 1) % count, i) for i in range(count)]),
            ],
            axis=dim,
        )
    return cells


def tables(length):
    indices = jnp.arange(length, dtype=jnp.int32)
    phases = indices[:, None] * indices[None, :] % length
    angles = phases.astype(jnp.float32) * (2.0 * math.pi / length)
    return (jnp.cos(angles), jnp.sin(angles))


def patches(padded, first_plane, planes):
    row_total = padded.shape[1]
    thickness = padded.shape[3]
    wrapped = jnp.concatenate([padded[:, -1:], padded, padded[:, :1]], axis=1)
    widened = jnp.pad(wrapped, ((0, 0), (0, 0), (0, 0), (1, 1)))
    pieces = []
    for step_first in (-1, 0, 1):
        for step_second in (-1, 0, 1):
            for step_third in (-1, 0, 1):
                pieces.append(
                    widened[
                        :,
                        1 + step_second : 1 + step_second + row_total,
                        first_plane + step_first : first_plane + step_first + planes,
                        1 + step_third : 1 + step_third + thickness,
                    ]
                )
    return jnp.stack(pieces)


def transform_rows(mesh_field, row_cosine, row_sine):
    real_part = jnp.einsum("cyxz,yk->ckxz", mesh_field, row_cosine, precision=HIGHEST)
    imag_part = -jnp.einsum("cyxz,yk->ckxz", mesh_field, row_sine, precision=HIGHEST)
    return jnp.stack([real_part, imag_part])


def transform_columns(stacked, col_cosine, col_sine, sign_value):

    def apply_table(part_values, table):
        return jnp.einsum("ckxz,xq->ckqz", part_values, table, precision=HIGHEST)

    real_part = stacked[0]
    imag_part = stacked[1]
    new_real = apply_table(real_part, col_cosine) + sign_value * apply_table(imag_part, col_sine)
    new_imag = apply_table(imag_part, col_cosine) - sign_value * apply_table(real_part, col_sine)
    return jnp.stack([new_real, new_imag])


def shards(atom_features, cotangent, cell_index, assign_weight, conv_kernel, spectral_gain):
    channels = atom_features.shape[1]
    slot_count = atom_features.shape[2] // NY
    own_planes = NX // lax.axis_size("brick")
    tile_cells = (own_planes + 2) * NZ
    snap_count = lax.axis_size("snap")
    index_tiles = cell_index[0].reshape(CORNERS, NY, slot_count)
    weight_tiles = assign_weight[0].astype(jnp.bfloat16).reshape(CORNERS, NY, slot_count)
    cell_numbers = jnp.arange(tile_cells, dtype=jnp.int32)
    blocks = jnp.zeros((NY, tile_cells, slot_count), jnp.bfloat16)
    for corner in range(CORNERS):
        matches = index_tiles[corner][:, None, :] == cell_numbers[None, :, None]
        blocks = blocks + jnp.where(
            matches, weight_tiles[corner][:, None, :], jnp.zeros((), jnp.bfloat16)
        )
    stacked = jnp.concatenate([atom_features[0], cotangent[0]], axis=0).reshape(
        2 * channels, NY, slot_count
    )
    spread = jnp.einsum("cts,tjs->ctj", stacked, blocks, preferred_element_type=jnp.float32)
    spread = spread.reshape(2 * channels, NY, own_planes + 2, NZ)
    from_above = from_behind(spread[:, :, 0], "brick", -1)
    from_below = from_behind(spread[:, :, own_planes + 1], "brick", 1)
    owned_planes = spread[:, :, 1 : own_planes + 1]
    owned_planes = owned_planes.at[:, :, 0].add(from_below)
    owned_planes = owned_planes.at[:, :, own_planes - 1].add(from_above)
    state_bf = owned_planes[:channels].astype(jnp.bfloat16)
    grad_mesh = owned_planes[channels:]
    col_cosine, col_sine = tables(NX)
    row_cosine, row_sine = tables(NY)

    def make_rows(mesh_field):
        return transform_rows(mesh_field, row_cosine, row_sine)

    def to_columns(part_rows):
        return transform_columns(part_rows, col_cosine, col_sine, 1.0)

    grad_rows = make_rows(grad_mesh)
    grad_spec = to_columns(
        lax.all_to_all(grad_rows, "brick", split_axis=2, concat_axis=3, tiled=True)
    )
    state_rim = with_halo(state_bf, (("brick", 2),), 1)
    state_patch = patches(state_rim, 1, own_planes)
    conv_out = jnp.einsum(
        "tcyxz,tcd->dyxz", state_patch, conv_kernel, preferred_element_type=jnp.float32
    )
    mesh_mixed = state_bf.astype(jnp.float32) + conv_out
    mixed_rows = make_rows(mesh_mixed)
    state_spec = to_columns(
        lax.all_to_all(
            mixed_rows.astype(jnp.bfloat16), "brick", split_axis=2, concat_axis=3, tiled=True
        ).astype(mixed_rows.dtype)
    )
    products = jnp.sum(grad_spec[0] * state_spec[0] + grad_spec[1] * state_spec[1], axis=3)
    gain_part = jnp.transpose(products, (0, 2, 1)) / (NX * NY * math.sqrt(snap_count * NZ))
    gain_local = jnp.transpose(spectral_gain, (0, 2, 1))
    filtered = grad_spec * gain_local[None, :, :, :, None]
    before_cross = transform_columns(filtered, col_cosine, col_sine, -1.0)
    part_cols = lax.all_to_all(before_cross, "brick", split_axis=3, concat_axis=2, tiled=True)
    real_rows = jnp.einsum("ckxz,ky->cyxz", part_cols[0], row_cosine, precision=HIGHEST)
    imag_rows = jnp.einsum("ckxz,ky->cyxz", part_cols[1], row_sine, precision=HIGHEST)
    grad_mixed = (real_rows - imag_rows) / (NX * NY)
    grad_bf = grad_mixed.astype(jnp.bfloat16)
    flipped = conv_kernel[::-1]
    grad_padded = with_halo(grad_bf, (("brick", 2),), 1)
    grad_patch = patches(grad_padded, 1, own_planes)
    back_conv = jnp.einsum(
        "tdyxz,tcd->cyxz", grad_patch, flipped, preferred_element_type=jnp.float32
    )
    pulled = (grad_bf.astype(jnp.float32) + back_conv).astype(jnp.bfloat16)
    pulled_full = with_halo(pulled, (("brick", 2),), 1)
    kernel_part = jnp.einsum(
        "tcyxz,dyxz->tcd", state_patch, grad_bf, preferred_element_type=jnp.float32
    )
    kernel_part = kernel_part / math.sqrt(snap_count * NX * NY * NZ)
    pulled_tiles = pulled_full.reshape(channels, NY, tile_cells)
    atom_total = jnp.einsum(
        "ctj,tjs->cts", pulled_tiles, blocks, preferred_element_type=jnp.float32
    )
    atom_grad = atom_total.astype(jnp.bfloat16).reshape(1, channels, NY * slot_count)
    kernel_grad = lax.psum(kernel_part, ("snap", "brick"))
    gain_grad = lax.psum(gain_part, "snap")
    return (atom_grad, kernel_grad, gain_grad)


BF = jnp.bfloat16
F32 = jnp.float32
LANES = 128
ROWS = 8
PADX = 16
MESH = pl.DeviceIdType.MESH


def contract(left, right, dims, precision=None):
    return lax.dot_general(
        left, right, ((dims[:1], dims[1:]), ((), ())),
        precision=precision, preferred_element_type=F32,
    )


def vmem():
    return pl.BlockSpec(memory_space=pltpu.VMEM)


def shape_of(dims, kind):
    return jax.ShapeDtypeStruct(dims, kind)


def corner_block(index_ref, weight_ref, lanes, cell_of_row):
    block = jnp.zeros(cell_of_row.shape, F32)
    index = index_ref[:, lanes]
    weight = weight_ref[:, lanes]
    for corner in range(CORNERS):
        block = jnp.where(
            index[corner : corner + 1] == cell_of_row, weight[corner : corner + 1], block
        )
    return block.astype(BF)


def row_cells():
    row = lax.broadcasted_iota(jnp.int32, (NZ * PADX, LANES), 0)
    return (row % PADX) * NZ + row // PADX


def run_all(first, total, make):
    def go(step, carry):
        make(step).start()
        return carry

    lax.fori_loop(first, total, go, 0)


def wait_all(first, total, make):
    def finish(step, carry):
        make(step).wait()
        return carry

    lax.fori_loop(first, total, finish, 0)


def split(value):
    high = value.astype(BF)
    return high, (value - high.astype(F32)).astype(BF)


def three(left, right):
    left_high, left_low = left
    right_high, right_low = right
    return (
        contract(left_high, right_high, (1, 0))
        + contract(left_high, right_low, (1, 0))
        + contract(left_low, right_high, (1, 0))
    )


def widen(value):
    return jnp.concatenate(
        [jnp.roll(value, 1, axis=0), value, jnp.roll(value, -1, axis=0)], axis=1
    ).astype(BF)


def whole_body(
    bricks, snaps, chunks,
    feature_hbm, cotangent_hbm, index_hbm, weight_hbm, taps_hbm, gain_hbm,
    order_hbm, rows_hbm, cols_hbm, inv_cols_hbm, inv_rows_hbm,
    atom_ref, kernel_ref, gain_out_ref,
    feature_ref, cotangent_ref, index_ref, weight_ref, taps_ref, gain_ref,
    order_ref, rows_ref, cols_ref, inv_cols_ref, inv_rows_ref,
    blocks, sums, edge, low, high, band, back_band, state, cat, grad_send, mixed_send,
    grad_slab, mixed_slab, gain_slab, field_f, back_f, spectra, ext, ret, back_cat, pulled,
    gain_out, gain_send, gain_pair, gain_both, part_all,
    kernel_part, kernel_land, kernel_mine, kernel_all,
    edge_sems, grad_sems, mixed_sems, gain_sems, ret_sems, part_sems, pair_sems, red_sems,
    in_sem, table_sem,
):
    channels = feature_ref.shape[0]
    planes = NX // bricks
    per = channels // bricks
    total = bricks * snaps
    me = lax.axis_index("brick")
    side = lax.axis_index("snap")
    flat = side * bricks + me
    above = lax.rem(me + 1, bricks)
    below = lax.rem(me + bricks - 1, bricks)
    barrier = pltpu.get_barrier_semaphore()

    def device_of(step):
        other = lax.rem(flat + step, total)
        return other, {"snap": other // bricks, "brick": lax.rem(other, bricks)}

    def hello(step, carry):
        pl.semaphore_signal(barrier, inc=1, device_id=device_of(step)[1], device_id_type=MESH)
        return carry

    def remote(src, dst, send_sem, recv_sem, device):
        return pltpu.make_async_remote_copy(
            src_ref=src, dst_ref=dst, send_sem=send_sem, recv_sem=recv_sem,
            device_id=device, device_id_type=MESH,
        )

    def partner(slot):
        return lax.rem(me + 1 + slot, bricks)

    def wait_for(src, dst, sems):
        remote(src, dst, sems[0], sems[1], {"brick": above}).wait()

    others = pl.ds(0, bricks - 1)
    span = NY // chunks
    tables = [
        pltpu.make_async_copy(src, dst, table_sem.at[number])
        for number, (src, dst) in enumerate(
            [
                (gain_hbm, gain_ref), (order_hbm, order_ref), (taps_hbm, taps_ref),
                (rows_hbm, rows_ref), (cols_hbm, cols_ref), (inv_cols_hbm, inv_cols_ref),
                (inv_rows_hbm, inv_rows_ref),
            ]
        )
    ]
    loads = []
    for chunk in range(chunks):
        lanes = pl.ds(chunk * span * LANES, span * LANES)
        loads.append(
            [
                pltpu.make_async_copy(src.at[:, lanes], dst.at[:, lanes], in_sem.at[number, chunk])
                for number, (src, dst) in enumerate(
                    [
                        (index_hbm, index_ref), (weight_hbm, weight_ref),
                        (feature_hbm, feature_ref), (cotangent_hbm, cotangent_ref),
                    ]
                )
            ]
        )
    for load in loads[0]:
        load.start()
    lax.fori_loop(1, total, hello, 0)
    for load in loads[1]:
        load.start()

    cells = row_cells()

    def spread_step(step, carry):
        parts = [[], []]
        for q in range(ROWS):
            y = step * ROWS + q
            lanes = pl.ds(pl.multiple_of(y * LANES, LANES), LANES)
            block = corner_block(index_ref, weight_ref, lanes, cells)
            blocks[y] = block
            stacked = jnp.concatenate([feature_ref[:, lanes], cotangent_ref[:, lanes]], axis=0)
            found = contract(block, stacked, (1, 1))
            for f in range(2):
                parts[f].append(
                    jnp.concatenate(
                        [
                            found[z * PADX : (z + 1) * PADX, f * channels : (f + 1) * channels]
                            for z in range(NZ)
                        ],
                        axis=1,
                    )
                )
        for f in range(2):
            turned = jnp.transpose(jnp.stack(parts[f]), (1, 0, 2))
            sums[f, :, pl.ds(pl.multiple_of(step * ROWS, ROWS), ROWS), :] = turned[: planes + 2]
        return carry

    def gain_copy(slot):
        target = partner(slot)
        return remote(
            gain_out.at[pl.ds(target * per, per)], gain_slab.at[:, me],
            gain_sems.at[0], gain_sems.at[1], {"brick": target},
        )

    def edge_copy(way):
        return remote(
            edge.at[pl.ds(2 * way, 2)], low if way == 0 else high,
            edge_sems.at[way, 0], edge_sems.at[way, 1], {"brick": above if way == 0 else below},
        )

    for chunk in range(chunks):
        for load in loads[chunk]:
            load.wait()
        if chunk + 2 < chunks:
            for load in loads[chunk + 2]:
                load.start()
        if chunk + 2 == chunks:
            for load in tables:
                load.start()
        if chunk == chunks - 1:
            tables[0].wait()
            gain_out[...] = gain_ref[...].astype(BF)
            gain_slab[:, me] = gain_out[pl.ds(me * per, per)]
            pl.semaphore_wait(barrier, total - 1)
            run_all(0, bricks - 1, gain_copy)
        lax.fori_loop(chunk * (span // ROWS), (chunk + 1) * (span // ROWS), spread_step, 0)
    for slot, plane in enumerate([planes, planes + 1, 0, 1]):
        edge[slot] = sums[0, plane].astype(BF)

    for way in range(2):
        edge_copy(way).start()
    tables[1].wait()
    order = order_ref[...]

    def place(field, out, plane):
        turned = contract(order, field.astype(BF), (1, 1))
        out[plane] = turned.reshape(out.shape[1:]).astype(BF)

    def field_copy(sems, send, slab):
        def make(slot):
            target = partner(slot)
            return remote(
                send.at[:, target], slab.at[me],
                sems.at[0], sems.at[1], {"brick": target},
            )

        return make

    grad_copy = field_copy(grad_sems, grad_send, grad_slab)
    def mixed_copy(first, count):
        some = pl.ds(first, count)

        def make(slot):
            target = partner(slot)
            return remote(
                mixed_send.at[some, target], mixed_slab.at[me, some],
                mixed_sems.at[0], mixed_sems.at[1], {"brick": target},
            )

        return make


    for plane in range(planes + 2):
        place(sums[1, plane], grad_send, plane)
    run_all(0, bricks - 1, grad_copy)
    grad_slab[me] = grad_send[:, me]

    tables[2].wait()
    lane = lax.broadcasted_iota(jnp.int32, (channels, LANES), 1) // channels
    for dx in range(3):
        for dy in range(3):
            tiled = []
            for dz in range(3):
                tap = taps_ref[9 * dx + 3 * dy + dz].astype(F32)
                tiled.append(jnp.concatenate([tap] * NZ, axis=1))
            lines = []
            for z in range(NZ):
                line = jnp.zeros((channels, LANES), F32)
                for dz in range(3):
                    line = jnp.where(lane == z - (dz - 1), tiled[dz], line)
                lines.append(line)
            square = jnp.concatenate(lines, axis=0)
            band[dx, dy * LANES : (dy + 1) * LANES, :] = square.astype(BF)
            back_band[2 - dx, (2 - dy) * LANES : (3 - dy) * LANES, :] = jnp.transpose(
                square, (1, 0)
            ).astype(BF)

    def settle(plane, value):
        rounded = value.astype(BF)
        state[plane] = rounded
        cat[plane] = widen(rounded.astype(F32))

    def convolve(plane):
        value = state[plane + 1].astype(F32)
        for dx in range(3):
            value = value + contract(cat[plane + dx], band[dx], (1, 0))
        place(value, mixed_send, plane)

    for plane in range(2, planes):
        settle(plane, sums[0, plane])
    for plane in range(2, planes - 2):
        convolve(plane)
    run_all(0, bricks - 1, mixed_copy(2, planes - 4))
    for way in range(2):
        edge_copy(way).wait()
    for plane in range(2):
        settle(plane, sums[0, plane] + low[plane].astype(F32))
        settle(planes + plane, sums[0, planes + plane] + high[plane].astype(F32))
    for plane in (0, 1, planes - 2, planes - 1):
        convolve(plane)
    run_all(0, bricks - 1, mixed_copy(0, 2))
    run_all(0, bricks - 1, mixed_copy(planes - 2, 2))
    mixed_slab[me] = mixed_send[:, me]

    for load in tables[3:]:
        load.wait()
    rows = rows_ref[...]
    cols = (cols_ref[0], cols_ref[1])
    inv_cols = (inv_cols_ref[0], inv_cols_ref[1])
    inv_rows = (inv_rows_ref[0], inv_rows_ref[1])

    def transform(channel):
        tall = jnp.concatenate([field_f[:, z * per + channel, :] for z in range(NZ)], axis=0)
        tall = tall.astype(BF)
        first = contract(jnp.concatenate([tall, tall], axis=1), rows, (1, 0))
        halves = []
        for half in range(2):
            halves.append(
                jnp.concatenate(
                    [
                        first[z * NX : (z + 1) * NX, half * NY : (half + 1) * NY]
                        for z in range(NZ)
                    ],
                    axis=1,
                )
            )
        return three(cols, split(jnp.concatenate(halves, axis=0)))

    wait_for(grad_send.at[:, others], grad_slab.at[others], (grad_sems.at[0], grad_sems.at[1]))
    for brick in range(bricks):
        field = grad_slab[brick].astype(F32)
        before = grad_slab[(brick + bricks - 1) % bricks, planes + 1].astype(F32)
        after = grad_slab[(brick + 1) % bricks, 0].astype(F32)
        field_f[pl.ds(brick * planes, planes)] = field[1 : planes + 1]
        field_f[brick * planes] = field[1] + before
        field_f[(brick + 1) * planes - 1] = field[planes] + after
    wait_for(gain_slab.at[:, others], gain_slab.at[:, others], (gain_sems.at[0], gain_sems.at[1]))
    for channel in range(per):
        spectra[channel] = transform(channel)
        gain = jnp.transpose(gain_slab[channel].astype(F32).reshape(NY, NX), (1, 0))
        gain = jnp.concatenate([gain] * NZ, axis=1)
        gain = jnp.concatenate([gain, gain], axis=0)
        back = three(inv_cols, split(spectra[channel] * gain))
        flats = []
        for z in range(NZ):
            piece = back[:, z * NY : (z + 1) * NY]
            flats.append(jnp.concatenate([piece[:NX], piece[NX:]], axis=1))
        out = three(split(jnp.concatenate(flats, axis=0)), inv_rows) * (1.0 / (NX * NY))
        for z in range(NZ):
            back_f[:, z * per + channel, :] = out[z * NX : (z + 1) * NX]
    ext[pl.ds(2, NX)] = back_f[...].astype(BF)
    ext[pl.ds(0, 2)] = back_f[pl.ds(NX - 2, 2)].astype(BF)
    ext[pl.ds(NX + 2, 2)] = back_f[pl.ds(0, 2)].astype(BF)

    def ret_copy(slot):
        target = partner(slot)
        return remote(
            ext.at[pl.ds(target * planes, planes + 4)], ret.at[:, me],
            ret_sems.at[0], ret_sems.at[1], {"brick": target},
        )

    run_all(0, bricks - 1, ret_copy)
    ret[:, me] = ext[pl.ds(me * planes, planes + 4)]

    wait_for(mixed_send.at[:, others], mixed_slab.at[others], (mixed_sems.at[0], mixed_sems.at[1]))
    field_f[...] = mixed_slab[...].reshape(field_f.shape).astype(F32)
    scale = 1.0 / (NX * NY * math.sqrt(snaps * NZ))
    for channel in range(per):
        product = spectra[channel] * transform(channel)
        product = product[:NX] + product[NX:]
        part = product[:, :NY]
        for z in range(1, NZ):
            part = part + product[:, z * NY : (z + 1) * NY]
        part = jnp.transpose(part * scale, (1, 0))
        gain_send[channel] = part.reshape(gain_send.shape[1:]).astype(gain_send.dtype)

    def part_copy(step):
        other, device = device_of(step)
        return remote(
            gain_send.at[other // bricks, lax.rem(other, bricks)], part_all.at[flat],
            part_sems.at[0], part_sems.at[1], device,
        )

    wait_for(ret.at[:, others], ret.at[:, others], (ret_sems.at[0], ret_sems.at[1]))
    for plane in range(planes + 4):
        field = ret[plane].astype(F32).reshape(LANES, NY).astype(BF)
        back_cat[plane] = widen(contract(field, order, (0, 0)))
    own = back_cat[pl.ds(2, planes)].reshape(planes * NY, 3 * LANES)
    groups = [jnp.zeros((channels, LANES), F32) for _ in range(kernel_all.shape[0] * ROWS // channels)]
    tap_scale = 1.0 / math.sqrt(snaps * NX * NY * NZ)
    for dx in range(3):
        near = state[pl.ds(dx, planes)].reshape(planes * NY, LANES)
        gram = contract(near, own, (0, 0))
        for dy in range(3):
            square = gram[:, (2 - dy) * LANES : (3 - dy) * LANES]
            for dz in range(3):
                line = jnp.zeros((channels, LANES), F32)
                for z in range(NZ):
                    source = z + dz - 1
                    if 0 <= source < NZ:
                        line = jnp.where(
                            lane == z, square[source * channels : (source + 1) * channels], line
                        )
                line = line + pltpu.roll(line, LANES // 2, 1)
                line = line + pltpu.roll(line, LANES // 4, 1)
                tap = 9 * dx + 3 * dy + dz
                groups[tap // NZ] = jnp.where(
                    lane == tap % NZ, line * tap_scale, groups[tap // NZ]
                )
    tiles = channels // ROWS
    for position, value in enumerate(groups):
        kernel_part[position * tiles : (position + 1) * tiles] = value.reshape(
            tiles, ROWS, LANES
        ).astype(BF)

    def scatter(step):
        other, device = device_of(step)
        return remote(
            kernel_part.at[other], kernel_land.at[flat],
            red_sems.at[0, 0], red_sems.at[0, 1], device,
        )

    def share(step):
        _, device = device_of(step)
        return remote(
            kernel_mine, kernel_all.at[flat], red_sems.at[1, 0], red_sems.at[1, 1], device,
        )

    run_all(1, total, scatter)
    kernel_land[flat] = kernel_part[flat]
    run_all(1, total, part_copy)
    part_all[flat] = gain_send[side, me]
    rest = pl.ds(0, total - 1)

    for plane in range(planes + 2):
        value = back_cat[plane + 1, :, LANES : 2 * LANES].astype(F32)
        for dx in range(3):
            value = value + contract(back_cat[plane + dx], back_band[dx], (1, 0))
        pulled[plane] = value.astype(BF).astype(F32)
    for plane in range(planes + 2, PADX):
        pulled[plane] = jnp.zeros((NY, LANES), F32)

    def gather_step(step, carry):
        here = pl.ds(pl.multiple_of(step * ROWS, ROWS), ROWS)
        turned = jnp.transpose(pulled[:, here, :], (1, 0, 2))
        for q in range(ROWS):
            y = step * ROWS + q
            lanes = pl.ds(pl.multiple_of(y * LANES, LANES), LANES)
            plane = turned[q]
            tall = jnp.concatenate(
                [plane[:, z * channels : (z + 1) * channels] for z in range(NZ)], axis=0
            )
            atom_ref[:, lanes] = contract(tall.astype(BF), blocks[y], (0, 0)).astype(BF)
        return carry

    steps = NY // ROWS
    lax.fori_loop(0, steps // 4, gather_step, 0)

    wait_for(kernel_land.at[rest], kernel_land.at[rest], (red_sems.at[0, 0], red_sems.at[0, 1]))
    kernel_mine[...] = jnp.sum(kernel_land[...].astype(F32), axis=0).astype(BF)
    run_all(1, total, share)
    kernel_all[flat] = kernel_mine[...]

    wait_for(part_all.at[rest], part_all.at[rest], (part_sems.at[0], part_sems.at[1]))
    gain_both[...] = part_all[pl.ds(0, bricks)].astype(F32) + part_all[pl.ds(bricks, bricks)].astype(F32)
    gain_swap = remote(
        gain_both, gain_pair, pair_sems.at[0], pair_sems.at[1], {"snap": snaps - 1 - side}
    )
    gain_swap.start()

    lax.fori_loop(steps // 4, steps, gather_step, 0)

    gain_swap.wait()
    for brick in range(bricks):
        gain_out_ref[brick * per + side] = gain_both[brick]
        gain_out_ref[brick * per + 1 - side] = gain_pair[brick]
    wait_for(kernel_all.at[rest], kernel_all.at[rest], (red_sems.at[1, 0], red_sems.at[1, 1]))
    final = kernel_all[...].astype(F32).reshape(kernel_all.shape[0] * ROWS // channels, channels, LANES)
    for tap in range(kernel_ref.shape[0]):
        at = (tap % NZ) * channels
        kernel_ref[tap] = final[tap // NZ][:, at : at + channels]


def fast_shards(sizes, atom_features, cotangent, cell_index, assign_weight, conv_kernel, spectral_gain):
    snaps, bricks = sizes
    channels, atoms = atom_features.shape[1:]
    planes = NX // bricks
    per = channels // bricks
    group = NZ * per
    total = bricks * snaps
    chunks = 4
    order = np.zeros((LANES, LANES), np.float32)
    for brick in range(bricks):
        for z in range(NZ):
            for c in range(per):
                order[brick * group + z * per + c, z * channels + brick * per + c] = 1.0

    def angles(length):
        phase = np.outer(np.arange(length), np.arange(length)) % length
        turn = 2.0 * np.pi * phase / length
        return np.cos(turn), np.sin(turn)

    def halves(table):
        table = np.asarray(table, np.float32)
        high = table.astype(BF)
        low = (table - high.astype(np.float32)).astype(BF)
        return high, low

    col_cos, col_sin = angles(NX)
    row_cos, row_sin = angles(NY)
    rows = jnp.asarray(np.concatenate(halves(np.concatenate([row_cos, -row_sin], axis=1)), axis=0))
    cols = jnp.asarray(np.stack(halves(np.block([[col_cos, col_sin], [-col_sin, col_cos]]))))
    inv_cols = jnp.asarray(np.stack(halves(np.block([[col_cos, -col_sin], [col_sin, col_cos]]))))
    inv_rows = jnp.asarray(np.stack(halves(np.concatenate([row_cos, -row_sin], axis=0))))
    mesh_plane = (NY, LANES)
    send = (planes, bricks, group, NY)
    slab = (NX, group, NY)
    piece = (bricks, NY // bricks, NX)
    scratch = [
        ((channels, atoms), BF),
        ((channels, atoms), BF),
        ((CORNERS, atoms), jnp.int32),
        ((CORNERS, atoms), F32),
        (conv_kernel.shape, BF),
        ((channels,) + piece[1:], F32),
        (order.shape, BF),
        (rows.shape, BF),
        (cols.shape, BF),
        (inv_cols.shape, BF),
        (inv_rows.shape, BF),
        ((NY, NZ * PADX, LANES), BF),
        ((2, planes + 2) + mesh_plane, F32),
        ((4,) + mesh_plane, BF),
        ((2,) + mesh_plane, BF),
        ((2,) + mesh_plane, BF),
        ((3, 3 * LANES, LANES), BF),
        ((3, 3 * LANES, LANES), BF),
        ((planes + 2,) + mesh_plane, BF),
        ((planes + 2, NY, 3 * LANES), BF),
        ((planes + 2,) + send[1:], BF),
        (send, BF),
        ((bricks, planes + 2) + slab[1:], BF),
        ((bricks, planes) + slab[1:], BF),
        ((per,) + piece, BF),
        (slab, F32),
        (slab, F32),
        ((per, 2 * NX, NZ * NY), F32),
        ((NX + 4, group, NY), BF),
        ((planes + 4, bricks, group, NY), BF),
        ((planes + 4, NY, 3 * LANES), BF),
        ((PADX,) + mesh_plane, F32),
        ((channels,) + piece[1:], BF),
        ((per,) + piece, BF),
        (piece, F32),
        (piece, F32),
        ((total,) + piece[1:], BF),
        ((total, ROWS, LANES), BF),
        ((total, ROWS, LANES), BF),
        ((ROWS, LANES), BF),
        ((total, ROWS, LANES), BF),
    ]
    sems = [(2, 2)] + [(2,)] * 6 + [(2, 2)] + [(4, chunks), (7,)]
    atom_grad, kernel_grad, gain_grad = pl.pallas_call(
        lambda *refs: whole_body(bricks, snaps, chunks, *refs),
        out_shape=[
            pltpu.VMEM((channels, atoms), BF),
            pltpu.VMEM(conv_kernel.shape, F32),
            pltpu.VMEM((channels,) + piece[1:], F32),
        ],
        in_specs=[pl.BlockSpec(memory_space=pl.ANY)] * 11,
        out_specs=[vmem()] * 3,
        scratch_shapes=[pltpu.VMEM(dims, kind) for dims, kind in scratch]
        + [pltpu.SemaphoreType.DMA(dims) for dims in sems],
        compiler_params=pltpu.CompilerParams(
            collective_id=1, has_side_effects=True, vmem_limit_bytes=60 * 1024 * 1024
        ),
    )(
        atom_features[0], cotangent[0], cell_index[0], assign_weight[0], conv_kernel,
        jnp.transpose(spectral_gain, (0, 2, 1)), jnp.asarray(order, BF), rows, cols,
        inv_cols, inv_rows,
    )
    return (atom_grad[None], kernel_grad, jnp.transpose(gain_grad, (0, 2, 1)))


def fits(mesh, channels, atoms):
    bricks = mesh.shape["brick"]
    snaps = mesh.shape["snap"]
    return (
        channels * NZ == LANES
        and NX == LANES
        and NY == LANES
        and atoms // bricks == NY * LANES
        and channels % bricks == 0
        and snaps == 2
        and NZ * channels // bricks == ROWS
        and NX // bricks == ROWS
        and 8 * channels == bricks * snaps * ROWS
    )


def solution(mesh):
    placed = (
        P("snap", None, "brick"),
        P("snap", None, "brick"),
        P("snap", None, "brick"),
        P("snap", None, "brick"),
        P(),
        P(None, None, "brick"),
    )
    sizes = (mesh.shape["snap"], mesh.shape["brick"])

    def pick(*arguments):
        if fits(mesh, arguments[0].shape[1], arguments[0].shape[2] * sizes[1]):
            return fast_shards(sizes, *arguments)
        return shards(*arguments)

    return jax.shard_map(
        pick,
        mesh=mesh,
        in_specs=placed,
        out_specs=(P("snap", None, "brick"), P(), P(None, None, "brick")),
        check_vma=False,
    )
```
